32 devices in a mesh: grp: 2 (over y), patch: 4 (over z), lead: 4 (over x, core).
Axes of the slice: x: 2, y: 2, z: 4, core: 2. Of those that a mesh axis runs over, the one named last changes fastest.
Arguments:
- features: bfloat16 [8, 4, 128, 32, 128], P(('grp', 'lead'), 'patch'), parts along dimension 0, may hold values from -6 to 6
- context: bfloat16 [4, 8, 128, 2048], P('patch', ('grp', 'lead')), parts along dimension 1, may hold values from -6 to 6
- owner: int32 [8], P('grp'), parts along dimension 0, may hold values from 0 to 3, as said below
- hours: int32 [8], P('grp'), parts along dimension 0, may hold values from 0 to 18, as said below
- w_first: bfloat16 [9, 192, 128], replicated, may hold values from -0.15625 to 0.15625
- w_second: bfloat16 [9, 128, 128], replicated, may hold values from -0.1875 to 0.1875
- w_lead_in: bfloat16 [128, 32], replicated, may hold values from -0.5 to 0.5
- w_lead_mix: bfloat16 [3, 32, 32], replicated, may hold values from -0.625 to 0.625
- w_lead_out: bfloat16 [32, 128], replicated, may hold values from -1 to 1
Outputs:
- updated: bfloat16 [8, 4, 128, 32, 128], P(('grp', 'lead'), 'patch'), parts along dimension 0
The draws below stay inside these ranges and needn't reach their ends.
There are 2 independent parts, one for each index of `grp`. The reference program is written for one: setup_inputs(seed, part) draws one part's arguments, and reference() takes and returns one part's arrays. A program takes and returns all parts, laid end to end along the dimension named above; an argument that names none is the same for every part. Nothing has to cross between parts.
Inputs may be any that keep to these rules, and one draw needn't show every extreme that they name: `owner`: values are patch indices; some lead hour is owned by patch 0 and some by patch 4 - 1. `hours`: strictly increasing along the lead hours; consecutive differences run from 1 to 6, both reached; the last lead hour is the largest value.
All inputs are finite; a program needn't handle non-finite values.
Results may differ from the reference program's by a relative error of at most 0.0037.
Values may be sent and summed in bfloat16 or wider, within the bound.
No kernel may reach another device: no remote copies, remote signals or barrier semaphores. Data moves between devices by JAX's collectives and lax.ppermute only.
A program may use at most 64 MiB of HBM per device.

```python
import jax
import jax.numpy as jnp
from jax import lax

H = 128
W = 32
CF = 128
CC = 64
CT = 32
LEADS = 4
PATCHES = 4


def draw_owner(key, part):
    picked = jax.random.randint(key, (LEADS,), 0, PATCHES)
    order = jax.random.permutation(jax.random.fold_in(key, 7), LEADS)
    picked = picked.at[order[0]].set(0)
    picked = picked.at[order[1]].set(PATCHES - 1)
    return picked.astype(jnp.int32)


def draw_hours(key, part):
    stride = jax.random.randint(key, (LEADS - 1,), 1, 7)
    order = jax.random.permutation(jax.random.fold_in(key, 11), LEADS - 1)
    stride = stride.at[order[0]].set(1)
    stride = stride.at[order[1]].set(6)
    rising = jnp.concatenate([jnp.zeros((1,), jnp.int32), jnp.cumsum(stride).astype(jnp.int32)])
    return (rising + 6 * (LEADS - 1) - rising[LEADS - 1]).astype(jnp.int32)


def block_scale(own_key, shape, cuts, least, high):
    loudness = 1.0
    for position, parts in cuts:
        draws = jax.random.uniform(jax.random.fold_in(jax.random.fold_in(own_key, 6), position), (parts,), jnp.float32, least / len(cuts), high / len(cuts))
        loudness = loudness * jnp.repeat(jnp.exp(draws), shape[position] // parts).reshape((-1,) + (1,) * (len(shape) - 1 - position))
    return loudness


def normal_values(stream_key, dims, scale, reach, pieces=(), held_as=jnp.bfloat16):
    values = scale * jax.random.normal(stream_key, dims, jnp.float32)
    if pieces:
        values = values * block_scale(stream_key, dims, pieces, -0.22, 0.18)
    return jnp.clip(values, -reach, reach).astype(held_as)


def setup_inputs(seed: int = 0, part: int = 0) -> dict:
    arg_keys = jax.random.split(jax.random.key(seed), 10)
    part_splits = jax.random.split(jax.random.fold_in(arg_keys[9], part), 10)
    features = normal_values(part_splits[0], (LEADS, PATCHES, H, W, CF), 1.0, 6.0, ((0, 4), (1, 4)))
    context = normal_values(part_splits[1], (PATCHES, LEADS, H, W * CC), 1.0, 6.0, ((0, 4), (1, 4)))
    owner = draw_owner(jax.random.fold_in(jax.random.fold_in(arg_keys[9], part), 71), part)
    hours = draw_hours(jax.random.fold_in(jax.random.fold_in(arg_keys[9], part), 71), part)
    w_first = normal_values(arg_keys[4], (9, CF + CC, CF), (9 * (CF + CC)) ** -0.5, 0.15625)
    w_second = normal_values(arg_keys[5], (9, CF, CF), (9 * CF) ** -0.5, 0.1875)
    w_lead_in = normal_values(arg_keys[6], (CF, CT), CF ** -0.5, 0.5)
    w_lead_mix = normal_values(arg_keys[7], (3, CT, CT), (3 * CT) ** -0.5, 0.625)
    w_lead_out = normal_values(arg_keys[8], (CT, CF), CT ** -0.5, 1.0)
    return dict(features=features, context=context, owner=owner, hours=hours, w_first=w_first, w_second=w_second, w_lead_in=w_lead_in, w_lead_mix=w_lead_mix, w_lead_out=w_lead_out)


def conv_padded(padded, kernel, height, width):
    depth = padded.shape[2]
    total = jnp.zeros((height * width, kernel.shape[2]), jnp.float32)
    for tap_index in range(9):
        row_off, col_off = divmod(tap_index, 3)
        window = padded[row_off:row_off + height, col_off:col_off + width].reshape(height * width, depth)
        total = total + jnp.dot(window, kernel[tap_index], preferred_element_type=jnp.float32)
    return total


def conv3x3(field, kernel):
    height, width = field.shape[0], field.shape[1]
    padded = jnp.pad(field, ((1, 1), (1, 1), (0, 0)))
    return conv_padded(padded, kernel, height, width)


def reference(features, context, owner, hours, w_first, w_second, w_lead_in, w_lead_mix, w_lead_out):
    lead_range = jnp.arange(LEADS, dtype=jnp.int32)
    chosen = context[owner, lead_range]
    lead_proj = jnp.dot(features.reshape(-1, CF), w_lead_in, preferred_element_type=jnp.float32).astype(jnp.bfloat16)
    lead_proj = lead_proj.reshape(LEADS, PATCHES, H * W, CT)
    lead_padded = jnp.pad(lead_proj, ((1, 1), (0, 0), (0, 0), (0, 0)))
    hour_float = hours.astype(jnp.float32)
    hour_gaps = hour_float[1:] - hour_float[:-1]
    gap_weight = jnp.exp(-0.5 * (hour_gaps - 1.0))
    zero_one = jnp.zeros((1,), jnp.float32)
    gain_prev = jnp.concatenate([zero_one, gap_weight])
    gain_next = jnp.concatenate([gap_weight, zero_one])

    def single(flat_index):
        lead_index = flat_index // PATCHES
        patch_index = flat_index % PATCHES
        resident = features[lead_index, patch_index]
        glob = chosen[lead_index].reshape(H, W, CC)
        joined = jnp.concatenate([resident, glob], axis=-1)
        first_pre = conv3x3(joined, w_first)
        first_act = jax.nn.silu(first_pre).astype(jnp.bfloat16).reshape(H, W, CF)
        second_pre = conv3x3(first_act, w_second)
        proj_prev = lead_padded[lead_index, patch_index]
        proj_self = lead_padded[lead_index + 1, patch_index]
        proj_next = lead_padded[lead_index + 2, patch_index]
        mixed = gain_prev[lead_index] * jnp.dot(proj_prev, w_lead_mix[0], preferred_element_type=jnp.float32)
        mixed = mixed + jnp.dot(proj_self, w_lead_mix[1], preferred_element_type=jnp.float32)
        mixed = mixed + gain_next[lead_index] * jnp.dot(proj_next, w_lead_mix[2], preferred_element_type=jnp.float32)
        mixed = mixed.astype(jnp.bfloat16)
        lifted = jnp.dot(mixed, w_lead_out, preferred_element_type=jnp.float32)
        result = resident.reshape(H * W, CF).astype(jnp.float32) + jax.nn.silu(second_pre + lifted)
        return result.astype(jnp.bfloat16).reshape(H, W, CF)

    updated = lax.map(single, jnp.arange(LEADS * PATCHES, dtype=jnp.int32))
    return updated.reshape(LEADS, PATCHES, H, W, CF)
```

```python
import jax
import jax.numpy as jnp
from jax import lax
from jax.experimental import pallas as pl
from jax.experimental.pallas import tpu as pltpu
from jax.sharding import PartitionSpec as P

BF16 = jnp.bfloat16
F32 = jnp.float32
EDGE = 8
CHUNK = 256
VMEM_BYTES = 40 * 1024 * 1024


def silu(v):
    return 0.5 * v * (1.0 + jnp.tanh(0.5 * v))


def dot(a, b):
    return jnp.dot(a, b, preferred_element_type=F32)


def in_vmem(count):
    return [pl.BlockSpec(memory_space=pltpu.VMEM)] * count


def put_pair_weights(target, weights, first, depth, offsets):
    out = weights.shape[2]
    span = depth * len(offsets)
    for a in range(3):
        for place, d in enumerate(offsets):
            rows = pl.ds(a * span + place * depth, depth)
            for q in range(2):
                b = d - q + 1
                lanes = pl.ds(q * out, out)
                if 0 <= b <= 2:
                    target[rows, lanes] = weights[3 * a + b, pl.ds(first, depth), :]
                else:
                    target[rows, lanes] = jnp.zeros((depth, out), target.dtype)


def clear_edges(ref, pairs):
    zero = jnp.zeros((pairs, ref.shape[1]), ref.dtype)
    ref[pl.ds(0, pairs), :] = zero
    ref[pl.ds(ref.shape[0] - pairs, pairs), :] = zero


def pair_taps(taps, weights, start, size, pairs):
    depth = taps.shape[1]
    total = dot(taps[pl.ds(start, size), :], weights[pl.ds(0, depth), :])
    for a in range(1, 3):
        total += dot(
            taps[pl.ds(start + a * pairs, size), :], weights[pl.ds(a * depth, depth), :]
        )
    return total


def column_masks(size, lanes, pairs):
    m = lax.broadcasted_iota(jnp.int32, (size, lanes), 0) & (pairs - 1)
    return m == 0, m == pairs - 1


def resident_kernel(
    x_ref, first_ref, second_ref, in_ref, acc_ref, proj_ref, w_second_ref, w_glob_ref,
    cells, taps, w_first, w_in,
):
    height, width, channels = x_ref.shape
    pairs = width // 2
    rows = height * pairs
    temporal = in_ref.shape[1]
    glob = first_ref.shape[1] - channels
    put_pair_weights(w_first, first_ref, 0, channels, (-1, 0, 1, 2))
    put_pair_weights(w_second_ref, second_ref, 0, channels, (-1, 0, 1, 2))
    put_pair_weights(w_glob_ref, first_ref, channels, glob, (0, 1, 2, -1))
    w_in[...] = jnp.zeros_like(w_in)
    for s in range(4):
        w_in[pl.ds(s * channels, channels), pl.ds(s * temporal, temporal)] = in_ref[...]
    clear_edges(taps, pairs)
    left, right = column_masks(CHUNK, channels, pairs)
    for start in range(0, rows, CHUNK):
        part = x_ref[pl.ds(start // pairs, CHUNK // pairs), :, :].astype(F32)
        cells[pl.ds(EDGE + 2 * start, 2 * CHUNK), :] = part.reshape(2 * CHUNK, channels)
    for start in range(0, rows, CHUNK):
        for place, d in enumerate((-1, 0, 1, 2)):
            value = cells[pl.ds(EDGE + 2 * start + d, CHUNK, stride=2), :]
            if d == -1:
                value = jnp.where(left, 0.0, value)
            if d == 2:
                value = jnp.where(right, 0.0, value)
            taps[pl.ds(pairs + start, CHUNK), pl.ds(place * channels, channels)] = value.astype(BF16)
    half = rows // 2
    for start in range(0, half, CHUNK):
        value = dot(
            taps[pl.ds(pairs + start, CHUNK), pl.ds(channels, 2 * channels)],
            w_in[pl.ds(0, 2 * channels), :],
        ) + dot(
            taps[pl.ds(pairs + half + start, CHUNK), pl.ds(channels, 2 * channels)],
            w_in[pl.ds(2 * channels, 2 * channels), :],
        )
        proj_ref[pl.ds(start, CHUNK), :] = value.astype(BF16)
    for start in range(0, rows, CHUNK):
        acc_ref[pl.ds(start, CHUNK), :] = pair_taps(taps, w_first, start, CHUNK, pairs)


def resident_part(x, w_first, w_second, w_in):
    height, width, channels = x.shape
    out = w_first.shape[2]
    temporal = w_in.shape[1]
    glob = w_first.shape[1] - channels
    pairs = width // 2
    rows = height * pairs
    return pl.pallas_call(
        resident_kernel,
        out_shape=(
            jax.ShapeDtypeStruct((rows, 2 * out), F32),
            jax.ShapeDtypeStruct((rows // 2, 4 * temporal), BF16),
            jax.ShapeDtypeStruct((12 * out, 2 * out), BF16),
            jax.ShapeDtypeStruct((12 * glob, 2 * out), BF16),
        ),
        in_specs=in_vmem(4),
        out_specs=tuple(in_vmem(4)),
        scratch_shapes=[
            pltpu.VMEM((2 * rows + 2 * EDGE, channels), F32),
            pltpu.VMEM((rows + 2 * pairs, 4 * channels), BF16),
            pltpu.VMEM((12 * channels, 2 * out), BF16),
            pltpu.VMEM((4 * channels, 4 * temporal), BF16),
        ],
        compiler_params=pltpu.CompilerParams(vmem_limit_bytes=VMEM_BYTES),
        cost_estimate=pl.CostEstimate(
            flops=2 * rows * 12 * channels * 2 * out,
            bytes_accessed=8 * 1024 * 1024,
            transcendentals=0,
        ),
        name="resident_part",
    )(x, w_first, w_second, w_in)


def mix_kernel(lead_axis, hours_ref, prev_ref, self_ref, next_ref, mix_ref, mixed_ref, w_mix):
    leads = hours_ref.shape[0]
    temporal = mix_ref.shape[1]
    lead = lax.axis_index(lead_axis)
    now = hours_ref[lead]
    before = hours_ref[jnp.maximum(lead - 1, 0)]
    after = hours_ref[jnp.minimum(lead + 1, leads - 1)]

    def gain(gap, used):
        gap = jnp.full((1, 4 * temporal), gap, jnp.int32).astype(F32)
        return jnp.where(used, jnp.exp(-0.5 * (gap - 1.0)), 0.0)

    gain_prev = gain(now - before, lead > 0)
    gain_next = gain(after - now, lead < leads - 1)
    w_mix[...] = jnp.zeros_like(w_mix)
    for k in range(3):
        for s in range(4):
            w_mix[k, pl.ds(s * temporal, temporal), pl.ds(s * temporal, temporal)] = mix_ref[k]
    rows = mixed_ref.shape[0]
    for start in range(0, rows, CHUNK):
        part = pl.ds(start, CHUNK)
        value = gain_prev * dot(prev_ref[part, :], w_mix[0])
        value = value + dot(self_ref[part, :], w_mix[1])
        value = value + gain_next * dot(next_ref[part, :], w_mix[2])
        mixed_ref[part, :] = value.astype(BF16)


def mix_part(hours, before, own, after, w_mix):
    lanes = own.shape[1]
    return pl.pallas_call(
        lambda *refs: mix_kernel("lead", *refs),
        out_shape=jax.ShapeDtypeStruct(own.shape, BF16),
        in_specs=[pl.BlockSpec(memory_space=pltpu.SMEM)] + in_vmem(4),
        out_specs=pl.BlockSpec(memory_space=pltpu.VMEM),
        scratch_shapes=[pltpu.VMEM((3, lanes, lanes), BF16)],
        cost_estimate=pl.CostEstimate(
            flops=6 * own.shape[0] * lanes * lanes, bytes_accessed=1024 * 1024, transcendentals=0
        ),
        name="mix_part",
    )(hours, before, own, after, w_mix)


def rest_kernel(
    place, owner_ref, acc_ref, x_ref, mixed_ref, w_second_ref, w_glob_ref, w_out_ref, *refs
):
    pieces, (out_ref, glob_cells, glob_taps, odd, even, taps, w_lift, cells) = refs[:-8], refs[-8:]
    height, width, channels = x_ref.shape
    pairs = width // 2
    rows = height * pairs
    out = channels
    temporal = w_out_ref.shape[0]
    lanes = glob_cells.shape[1]
    share = height // len(pieces)
    clear_edges(glob_taps, pairs)
    clear_edges(taps, pairs)
    w_lift[...] = jnp.zeros_like(w_lift)
    for s in range(2):
        for q in range(2):
            w_lift[
                s, pl.ds((2 * s + q) * temporal, temporal), pl.ds(q * out, out)
            ] = w_out_ref[...]
    for k, piece in enumerate(pieces):
        base = place(owner_ref, k) * (share * pairs)
        for m in range(pairs):
            value = piece[:, pl.ds(m * lanes, lanes)].astype(F32)
            glob_cells[pl.ds(EDGE + base + m, share, stride=pairs), :] = value
    left, right = column_masks(CHUNK, lanes, pairs)
    low = lax.broadcasted_iota(jnp.int32, (CHUNK, lanes), 1) < lanes // 2
    for start in range(0, rows, CHUNK):
        here = glob_cells[pl.ds(EDGE + start, CHUNK), :]
        before = jnp.where(left, 0.0, glob_cells[pl.ds(EDGE + start - 1, CHUNK), :])
        after = jnp.where(right, 0.0, glob_cells[pl.ds(EDGE + start + 1, CHUNK), :])
        glob_taps[pl.ds(pairs + start, CHUNK), pl.ds(0, lanes)] = here.astype(BF16)
        glob_taps[pl.ds(pairs + start, CHUNK), pl.ds(lanes, lanes)] = jnp.where(
            low, after, before
        ).astype(BF16)
    for start in range(0, rows, CHUNK):
        value = acc_ref[pl.ds(start, CHUNK), :] + pair_taps(
            glob_taps, w_glob_ref, start, CHUNK, pairs
        )
        value = silu(value)
        even[pl.ds(EDGE + start, CHUNK), :] = value[:, :out]
        odd[pl.ds(EDGE + start, CHUNK), :] = value[:, out:]
        taps[pl.ds(pairs + start, CHUNK), pl.ds(out, 2 * out)] = value.astype(BF16)
    left, right = column_masks(CHUNK, out, pairs)
    for start in range(0, rows, CHUNK):
        before = jnp.where(left, 0.0, odd[pl.ds(EDGE + start - 1, CHUNK), :])
        after = jnp.where(right, 0.0, even[pl.ds(EDGE + start + 1, CHUNK), :])
        taps[pl.ds(pairs + start, CHUNK), pl.ds(0, out)] = before.astype(BF16)
        taps[pl.ds(pairs + start, CHUNK), pl.ds(3 * out, out)] = after.astype(BF16)
    half = rows // 2
    for start in range(0, rows, CHUNK):
        s = start // half
        value = pair_taps(taps, w_second_ref, start, CHUNK, pairs)
        value = value + dot(mixed_ref[pl.ds(start - s * half, CHUNK), :], w_lift[s])
        value = silu(value)
        cells[pl.ds(2 * start, CHUNK, stride=2), :] = value[:, :out]
        cells[pl.ds(2 * start + 1, CHUNK, stride=2), :] = value[:, out:]
        part = pl.ds(start // pairs, CHUNK // pairs)
        value = cells[pl.ds(2 * start, 2 * CHUNK), :].reshape(CHUNK // pairs, width, channels)
        out_ref[part, :, :] = (x_ref[part, :, :].astype(F32) + value).astype(BF16)


def rest_part(place, owner, acc, x, mixed, w_second, w_glob, w_out, pieces):
    height, width, channels = x.shape
    pairs = width // 2
    rows = height * pairs
    lanes = pieces[0].shape[1] // pairs
    return pl.pallas_call(
        lambda *refs: rest_kernel(place, *refs),
        out_shape=jax.ShapeDtypeStruct(x.shape, BF16),
        in_specs=[pl.BlockSpec(memory_space=pltpu.SMEM)] + in_vmem(6 + len(pieces)),
        out_specs=pl.BlockSpec(memory_space=pltpu.VMEM),
        scratch_shapes=[
            pltpu.VMEM((rows + 2 * EDGE, lanes), F32),
            pltpu.VMEM((rows + 2 * pairs, 2 * lanes), BF16),
            pltpu.VMEM((rows + 2 * EDGE, channels), F32),
            pltpu.VMEM((rows + 2 * EDGE, channels), F32),
            pltpu.VMEM((rows + 2 * pairs, 4 * channels), BF16),
            pltpu.VMEM((2, mixed.shape[1], 2 * channels), BF16),
            pltpu.VMEM((2 * rows, channels), F32),
        ],
        compiler_params=pltpu.CompilerParams(vmem_limit_bytes=VMEM_BYTES),
        cost_estimate=pl.CostEstimate(
            flops=4 * rows * 12 * channels * 2 * channels,
            bytes_accessed=8 * 1024 * 1024,
            transcendentals=0,
        ),
        name="rest_part",
    )(owner, acc, x, mixed, w_second, w_glob, w_out, *pieces)


def passed_along(block, axis, distance):
    devices = range(lax.axis_size(axis))
    route = [(i - distance, i) for i in devices if i - distance in devices]
    return lax.ppermute(block, axis, route)


def rotated(block, axis, distance):
    count = lax.axis_size(axis)
    return lax.ppermute(block, axis, [(i, (i + distance) % count) for i in range(count)])


def pick_kernel(owner_ref, *refs):
    pieces, out_ref = refs[:-1], refs[-1]
    count = len(pieces)
    want = lax.rem(
        lax.axis_index("patch") - owner_ref[lax.axis_index("lead")] + count, count
    )
    for k, piece in enumerate(pieces):

        @pl.when(want == k)
        def _(piece=piece):
            out_ref[...] = piece[...]


def pick(owner, pieces):
    return pl.pallas_call(
        pick_kernel,
        out_shape=jax.ShapeDtypeStruct(pieces[0].shape, pieces[0].dtype),
        in_specs=[pl.BlockSpec(memory_space=pltpu.SMEM)] + in_vmem(len(pieces)),
        out_specs=pl.BlockSpec(memory_space=pltpu.VMEM),
        name="pick",
    )(owner, *pieces)


def spread(block, owner):
    count = lax.axis_size("patch")
    share = block.shape[0] // count
    pieces = [block[k * share : (k + 1) * share] for k in range(count)]
    got = [pieces[0]] + [rotated(pieces[k], "patch", k) for k in range(1, count)]
    held = pick(owner, got)
    held_by = [held] + [rotated(held, "patch", k) for k in range(1, count)]

    def place(owner_ref, k):
        away = lax.axis_index("patch") - k - owner_ref[lax.axis_index("lead")]
        return lax.rem(away + 2 * count, count)

    return held_by, place


def broadcast(block, owner):
    mine = lax.axis_index("patch") == owner[lax.axis_index("lead")]
    block = lax.psum(jnp.where(mine, block, jnp.zeros_like(block)), "patch")
    return [block], lambda owner_ref, k: 0


def per_device(
    features, context, owner, hours, w_first, w_second, w_lead_in, w_lead_mix, w_lead_out
):
    resident = features[0, 0]
    few = lax.axis_size("patch") <= 4
    pieces, place = (spread if few else broadcast)(context[0, 0], owner)
    acc, proj, w_second, w_glob = resident_part(resident, w_first, w_second, w_lead_in)
    preceding = passed_along(proj, "lead", 1)
    following = passed_along(proj, "lead", -1)
    mixed = mix_part(hours, preceding, proj, following, w_lead_mix)
    result = rest_part(place, owner, acc, resident, mixed, w_second, w_glob, w_lead_out, pieces)
    return result[None, None]


def solution(mesh):
    placed = (
        P(("grp", "lead"), "patch", None, None, None),
        P("patch", ("grp", "lead"), None, None),
        P("grp"),
        P("grp"),
        P(),
        P(),
        P(),
        P(),
        P(),
    )
    return jax.shard_map(
        per_device,
        mesh=mesh,
        in_specs=placed,
        out_specs=P(("grp", "lead"), "patch", None, None, None),
        check_vma=False,
    )
```

```python
import jax
import jax.numpy as jnp
from jax import lax
from jax.experimental import pallas as pl
from jax.experimental.pallas import tpu as pltpu
from jax.sharding import PartitionSpec as P

BF16 = jnp.bfloat16
F32 = jnp.float32
EDGE = 8
CHUNK = 256
WIDE = 1024
GROUPS = 1
VMEM_BYTES = 20 * 1024 * 1024


def silu(v):
    return 0.5 * v * (1.0 + jnp.tanh(0.5 * v))


def dot(a, b):
    return jnp.dot(a, b, preferred_element_type=F32)


def dot_transposed(a, b):
    return lax.dot_general(a, b, (((1,), (1,)), ((), ())), preferred_element_type=F32)


def in_vmem(count):
    return [pl.BlockSpec(memory_space=pltpu.VMEM)] * count


def in_hbm(count):
    return [pl.BlockSpec(memory_space=pltpu.HBM)] * count


def start_copies(pairs, sems):
    copies = [
        pltpu.make_async_copy(source, target, sems.at[k])
        for k, (source, target) in enumerate(pairs)
    ]
    for copy in copies:
        copy.start()
    return copies


def put_pair_weights(target, weights, first, depth, offsets):
    out = weights.shape[2]
    span = depth * len(offsets)
    for a in range(3):
        for place, d in enumerate(offsets):
            rows = pl.ds(a * span + place * depth, depth)
            for q in range(2):
                b = d - q + 1
                lanes = pl.ds(q * out, out)
                if 0 <= b <= 2:
                    target[rows, lanes] = weights[3 * a + b, pl.ds(first, depth), :]
                else:
                    target[rows, lanes] = jnp.zeros((depth, out), target.dtype)


def clear_edges(ref, pairs):
    zero = jnp.zeros((pairs, ref.shape[1]), ref.dtype)
    ref[pl.ds(0, pairs), :] = zero
    ref[pl.ds(ref.shape[0] - pairs, pairs), :] = zero


def pair_taps(taps, weights, start, size, pairs):
    depth = taps.shape[1]
    total = dot(taps[pl.ds(start, size), :], weights[pl.ds(0, depth), :])
    for a in range(1, 3):
        total += dot(
            taps[pl.ds(start + a * pairs, size), :], weights[pl.ds(a * depth, depth), :]
        )
    return total


def column_masks(size, lanes, pairs):
    m = lax.rem(lax.broadcasted_iota(jnp.int32, (size, lanes), 0), pairs)
    return m == 0, m == pairs - 1


def looped(count, body):
    lax.fori_loop(0, count, lambda k, carry: (body(k), carry)[1], 0)


def resident_kernel(
    x_hbm, first_hbm, second_hbm, w_in_hbm, acc_ref, proj_ref, w_second_hbm, w_glob_hbm,
    x_ref, first_ref, second_ref, in_ref, w_second_ref, w_glob_ref, cells, taps, w_first, w_in, sems,
):
    height, width, channels = x_ref.shape
    pairs = width // 2
    rows = height * pairs
    temporal = in_ref.shape[0]
    glob = first_ref.shape[1] - channels
    copies = start_copies(
        [(x_hbm, x_ref), (w_in_hbm, in_ref), (first_hbm, first_ref), (second_hbm, second_ref)],
        sems,
    )
    clear_edges(taps, pairs)
    w_in[...] = jnp.zeros_like(w_in)
    left, right = column_masks(CHUNK, channels, pairs)
    copies[0].wait()
    for start in range(0, rows, CHUNK):
        part = x_ref[pl.ds(start // pairs, CHUNK // pairs), :, :].astype(F32)
        cells[pl.ds(EDGE + 2 * start, 2 * CHUNK), :] = part.reshape(2 * CHUNK, channels)
    for start in range(0, rows, CHUNK):
        for place, d in enumerate((-1, 0, 1, 2)):
            value = cells[pl.ds(EDGE + 2 * start + d, CHUNK, stride=2), :]
            if d == -1:
                value = jnp.where(left, 0.0, value)
            if d == 2:
                value = jnp.where(right, 0.0, value)
            taps[pl.ds(pairs + start, CHUNK), pl.ds(place * channels, channels)] = value.astype(BF16)
    half = rows // 2
    copies[1].wait()
    for s in range(4):
        w_in[pl.ds(s * temporal, temporal), pl.ds(s * channels, channels)] = in_ref[...]
    for start in range(0, half, CHUNK):
        value = dot_transposed(
            taps[pl.ds(pairs + start, CHUNK), pl.ds(channels, 2 * channels)],
            w_in[:, pl.ds(0, 2 * channels)],
        ) + dot_transposed(
            taps[pl.ds(pairs + half + start, CHUNK), pl.ds(channels, 2 * channels)],
            w_in[:, pl.ds(2 * channels, 2 * channels)],
        )
        proj_ref[pl.ds(start, CHUNK), :] = value.astype(BF16)
    copies[2].wait()
    put_pair_weights(w_first, first_ref, 0, channels, (-1, 0, 1, 2))
    put_pair_weights(w_glob_ref, first_ref, channels, glob, (0, 1, 2, -1))
    copies[3].wait()
    put_pair_weights(w_second_ref, second_ref, 0, channels, (-1, 0, 1, 2))
    writes = start_copies(
        [(w_glob_ref, w_glob_hbm), (w_second_ref, w_second_hbm)], sems.at[pl.ds(4, 2)]
    )
    for start in range(0, rows, WIDE):
        acc_ref[pl.ds(start, WIDE), :] = pair_taps(taps, w_first, start, WIDE, pairs)
    for write in writes:
        write.wait()


def resident_part(x, w_first, w_second, w_in):
    height, width, channels = x.shape
    out = w_first.shape[2]
    temporal = w_in.shape[1]
    w_in = w_in.T
    glob = w_first.shape[1] - channels
    pairs = width // 2
    rows = height * pairs
    results = (
        ((rows, 2 * out), F32),
        ((rows // 2, 4 * temporal), BF16),
        ((12 * out, 2 * out), BF16),
        ((12 * glob, 2 * out), BF16),
    )
    return pl.pallas_call(
        resident_kernel,
        out_shape=tuple(
            space(*kind) for space, kind in zip((pltpu.VMEM,) * 2 + (pltpu.HBM,) * 2, results)
        ),
        in_specs=in_hbm(4),
        out_specs=tuple(in_vmem(2) + in_hbm(2)),
        scratch_shapes=[
            pltpu.VMEM(x.shape, BF16),
            pltpu.VMEM(w_first.shape, BF16),
            pltpu.VMEM(w_second.shape, BF16),
            pltpu.VMEM(w_in.shape, BF16),
            pltpu.VMEM(*results[2]),
            pltpu.VMEM(*results[3]),
            pltpu.VMEM((2 * rows + 2 * EDGE, channels), F32),
            pltpu.VMEM((rows + 2 * pairs, 4 * channels), BF16),
            pltpu.VMEM((12 * channels, 2 * out), BF16),
            pltpu.VMEM((4 * temporal, 4 * channels), BF16),
            pltpu.SemaphoreType.DMA((6,)),
        ],
        compiler_params=pltpu.CompilerParams(vmem_limit_bytes=VMEM_BYTES),
        cost_estimate=pl.CostEstimate(flops=1024, bytes_accessed=1024, transcendentals=0),
        name="resident_part",
    )(*(pltpu.with_memory_space_constraint(a, pltpu.HBM) for a in (x, w_first, w_second, w_in)))


def mix_kernel(hours_ref, prev_ref, self_ref, next_ref, mix_ref, mixed_ref, w_mix):
    leads = hours_ref.shape[0]
    temporal = mix_ref.shape[1]
    lead = lax.axis_index("lead")
    now = hours_ref[lead]
    before = hours_ref[jnp.maximum(lead - 1, 0)]
    after = hours_ref[jnp.minimum(lead + 1, leads - 1)]

    def gain(gap, used):
        gap = jnp.full((1, 4 * temporal), gap, jnp.int32).astype(F32)
        return jnp.where(used, jnp.exp(-0.5 * (gap - 1.0)), 0.0)

    gain_prev = gain(now - before, lead > 0)
    gain_next = gain(after - now, lead < leads - 1)
    w_mix[...] = jnp.zeros_like(w_mix)
    for k in range(3):
        for s in range(4):
            w_mix[k, pl.ds(s * temporal, temporal), pl.ds(s * temporal, temporal)] = mix_ref[k]
    rows = mixed_ref.shape[0]
    for start in range(0, rows, CHUNK):
        part = pl.ds(start, CHUNK)
        value = gain_prev * dot(prev_ref[part, :], w_mix[0])
        value = value + dot(self_ref[part, :], w_mix[1])
        value = value + gain_next * dot(next_ref[part, :], w_mix[2])
        mixed_ref[part, :] = value.astype(BF16)


def mix_part(hours, before, own, after, w_mix):
    lanes = own.shape[1]
    return pl.pallas_call(
        mix_kernel,
        out_shape=jax.ShapeDtypeStruct(own.shape, BF16),
        in_specs=[pl.BlockSpec(memory_space=pltpu.SMEM)] + in_vmem(4),
        out_specs=in_vmem(1)[0],
        scratch_shapes=[
            pltpu.VMEM((3, lanes, lanes), BF16),
        ],
        compiler_params=pltpu.CompilerParams(vmem_limit_bytes=VMEM_BYTES),
        cost_estimate=pl.CostEstimate(
            flops=6 * own.shape[0] * lanes * lanes, bytes_accessed=1024 * 1024, transcendentals=0
        ),
        name="mix_part",
    )(hours, before, own, after, w_mix)


def rest_kernel(
    place, owner_ref, acc_ref, mixed_ref, x_hbm, w_second_hbm, w_glob_hbm, w_out_hbm, *refs
):
    pieces, refs = refs[:-14], refs[-14:]
    out_hbm, x_ref, w_second_ref, w_glob_ref, w_out_ref, *refs = refs
    out_ref, glob_cells, glob_taps, odd, even, taps, w_lift, cells, sems = refs
    copies = start_copies(
        [
            (w_glob_hbm, w_glob_ref),
            (w_out_hbm, w_out_ref),
            (w_second_hbm, w_second_ref),
            (x_hbm, x_ref),
        ],
        sems,
    )
    height, width, channels = x_ref.shape
    pairs = width // 2
    rows = height * pairs
    out = channels
    temporal = w_out_ref.shape[0]
    lanes = glob_cells.shape[1]
    share = pieces[0].shape[0]
    chunks = rows // CHUNK
    wide = rows // WIDE

    def out_copy(k):
        part = pl.ds(k * (WIDE // pairs), WIDE // pairs)
        return pltpu.make_async_copy(
            out_ref.at[part, :, :], out_hbm.at[part, :, :], sems.at[4 + k]
        )

    clear_edges(glob_taps, pairs)
    clear_edges(taps, pairs)
    w_lift[...] = jnp.zeros_like(w_lift)
    for k, piece in enumerate(pieces):
        base = EDGE + place(owner_ref, k) * (share * pairs)
        for m in range(pairs):
            value = piece[:, pl.ds(m * lanes, lanes)].astype(F32)
            glob_cells[pl.ds(base + m, share, stride=pairs), :] = value
    left, right = column_masks(CHUNK, lanes, pairs)
    lower = lax.broadcasted_iota(jnp.int32, (CHUNK, lanes), 1) < lanes // 2

    def glob_chunk(k):
        start = pl.multiple_of(k * CHUNK, CHUNK)
        here = glob_cells[pl.ds(EDGE + start, CHUNK), :]
        before = jnp.where(left, 0.0, glob_cells[pl.ds(EDGE - 1 + start, CHUNK), :])
        after = jnp.where(right, 0.0, glob_cells[pl.ds(EDGE + 1 + start, CHUNK), :])
        part = pl.ds(pairs + start, CHUNK)
        glob_taps[part, pl.ds(0, lanes)] = here.astype(BF16)
        glob_taps[part, pl.ds(lanes, lanes)] = jnp.where(lower, after, before).astype(BF16)

    looped(chunks, glob_chunk)
    for copy in copies[:2]:
        copy.wait()
    for s in range(2):
        for q in range(2):
            w_lift[
                s, pl.ds((2 * s + q) * temporal, temporal), pl.ds(q * out, out)
            ] = w_out_ref[...]
    left, right = column_masks(WIDE, out, pairs)

    def act_chunk(k):
        start = pl.multiple_of(k * WIDE, WIDE)
        value = acc_ref[pl.ds(start, WIDE), :] + pair_taps(
            glob_taps, w_glob_ref, start, WIDE, pairs
        )
        value = silu(value)
        even[pl.ds(EDGE + start, WIDE), :] = value[:, :out]
        odd[pl.ds(EDGE + start, WIDE), :] = value[:, out:]
        part = pl.ds(pairs + start, WIDE)
        taps[part, pl.ds(out, 2 * out)] = value.astype(BF16)
        before = jnp.where(left, 0.0, odd[pl.ds(EDGE - 1 + start, WIDE), :])
        after = jnp.where(right, 0.0, even[pl.ds(EDGE + 1 + start, WIDE), :])
        taps[part, pl.ds(0, out)] = before.astype(BF16)
        taps[part, pl.ds(3 * out, out)] = after.astype(BF16)

    looped(wide, act_chunk)
    for copy in copies[2:]:
        copy.wait()

    def out_chunk(k):
        start = pl.multiple_of(k * WIDE, WIDE)
        s = lax.div(2 * k, wide)
        value = pair_taps(taps, w_second_ref, start, WIDE, pairs)
        low = pl.multiple_of(start - s * (rows // 2), WIDE)
        value = value + dot(mixed_ref[pl.ds(low, WIDE), :], w_lift[s])
        value = silu(value)
        cells[pl.ds(2 * start, WIDE, stride=2), :] = value[:, :out]
        cells[pl.ds(2 * start + 1, WIDE, stride=2), :] = value[:, out:]
        part = pl.ds(k * (WIDE // pairs), WIDE // pairs)
        value = cells[pl.ds(2 * start, 2 * WIDE), :].reshape(WIDE // pairs, width, channels)
        out_ref[part, :, :] = (x_ref[part, :, :].astype(F32) + value).astype(BF16)
        out_copy(k).start()

    looped(wide, out_chunk)
    for k in range(wide):
        out_copy(k).wait()


def rest_part(place, owner, acc, x, mixed, w_second, w_glob, w_out, pieces):
    height, width, channels = x.shape
    pairs = width // 2
    rows = height * pairs
    lanes = pieces[0].shape[1] // pairs
    loaded = [x, w_second, w_glob, w_out]
    return pl.pallas_call(
        lambda *refs: rest_kernel(place, *refs),
        out_shape=jax.ShapeDtypeStruct(x.shape, BF16),
        in_specs=[pl.BlockSpec(memory_space=pltpu.SMEM)]
        + in_vmem(2)
        + in_hbm(len(loaded))
        + in_vmem(len(pieces)),
        out_specs=in_hbm(1)[0],
        scratch_shapes=[
            *(pltpu.VMEM(a.shape, a.dtype) for a in loaded),
            pltpu.VMEM(x.shape, BF16),
            pltpu.VMEM((rows + 2 * EDGE, lanes), F32),
            pltpu.VMEM((rows + 2 * pairs, 2 * lanes), BF16),
            pltpu.VMEM((rows + 2 * EDGE, channels), F32),
            pltpu.VMEM((rows + 2 * EDGE, channels), F32),
            pltpu.VMEM((rows + 2 * pairs, 4 * channels), BF16),
            pltpu.VMEM((2, mixed.shape[1], 2 * channels), BF16),
            pltpu.VMEM((2 * rows, channels), F32),
            pltpu.SemaphoreType.DMA((4 + rows // WIDE,)),
        ],
        compiler_params=pltpu.CompilerParams(vmem_limit_bytes=VMEM_BYTES),
        cost_estimate=pl.CostEstimate(
            flops=4 * rows * 12 * channels * 2 * channels,
            bytes_accessed=8 * 1024 * 1024,
            transcendentals=0,
        ),
        name="rest_part",
    )(
        owner,
        pltpu.with_memory_space_constraint(acc, pltpu.VMEM),
        mixed,
        *(pltpu.with_memory_space_constraint(a, pltpu.HBM) for a in loaded),
        *pieces,
    )


def rotated(block, axis, distance):
    count = lax.axis_size(axis)
    return lax.ppermute(block, axis, [(i, (i + distance) % count) for i in range(count)])


def swapped(block, bit):
    count = lax.axis_size("patch")
    return lax.ppermute(block, "patch", [(i, i ^ bit) for i in range(count)])


def spread(block, owner, early):
    away = lax.axis_index("patch") ^ owner[lax.axis_index("lead")]
    near, beside = (away & 1) == 0, (away & 2) == 0
    half = block.shape[0] // 2
    share = half // (2 * GROUPS)
    arrived, early = lax.optimization_barrier((swapped(block[half:], 1), early))
    pieces = []
    for g in range(GROUPS):
        rows = slice(2 * g * share, 2 * (g + 1) * share)
        part = jnp.where(near, block[rows], arrived[rows])
        own = jnp.where(beside, part[:share], swapped(part[share:], 2))
        across = swapped(own, 2)
        pieces += [own, swapped(own, 1), across, swapped(across, 1)]
    return pieces, early


def piece_place(owner_ref, k):
    away = lax.axis_index("patch") ^ owner_ref[lax.axis_index("lead")] ^ (k % 4)
    return (away & 1) * (2 * GROUPS) + 2 * (k // 4) + (away >> 1)


def whole_place(owner_ref, k):
    return 0


def per_device(
    features, context, owner, hours, w_first, w_second, w_lead_in, w_lead_mix, w_lead_out
):
    resident = features[0, 0]
    height = resident.shape[0]
    count = lax.axis_size("patch")
    acc, proj, w_second, w_glob = resident_part(resident, w_first, w_second, w_lead_in)
    constants = (w_second, w_glob, w_lead_out)

    def mixed_with(proj):
        return mix_part(
            hours, rotated(proj, "lead", 1), proj, rotated(proj, "lead", -1), w_lead_mix
        )

    if count == 4:
        pieces, proj = spread(context[0, 0], owner, proj)
        place = piece_place
    else:
        mine = lax.axis_index("patch") == owner[lax.axis_index("lead")]
        block = jnp.where(mine, context[0, 0], jnp.zeros_like(context[0, 0]))
        pieces, place = [lax.psum(block, "patch")], whole_place
    result = rest_part(place, owner, acc, resident, mixed_with(proj), *constants, pieces)
    return result[None, None]


def solution(mesh):
    placed = (
        P(("grp", "lead"), "patch", None, None, None),
        P("patch", ("grp", "lead"), None, None),
        P("grp"),
        P("grp"),
        P(),
        P(),
        P(),
        P(),
        P(),
    )
    return jax.shard_map(
        per_device,
        mesh=mesh,
        in_specs=placed,
        out_specs=P(("grp", "lead"), "patch", None, None, None),
        check_vma=False,
    )
```

```python
import jax
import jax.numpy as jnp
from jax import lax
from jax.experimental import pallas as pl
from jax.experimental.pallas import tpu as pltpu
from jax.sharding import PartitionSpec as P

BF16 = jnp.bfloat16
F32 = jnp.float32
EDGE = 8
CHUNK = 256
WIDE = 1024
GROUPS = 1
VMEM_BYTES = 20 * 1024 * 1024


def silu(v):
    return 0.5 * v * (1.0 + jnp.tanh(0.5 * v))


def dot(a, b):
    return jnp.dot(a, b, preferred_element_type=F32)


def dot_transposed(a, b):
    return lax.dot_general(a, b, (((1,), (1,)), ((), ())), preferred_element_type=F32)


def in_vmem(count):
    return [pl.BlockSpec(memory_space=pltpu.VMEM)] * count


def at_hbm(*arrays):
    return [pltpu.with_memory_space_constraint(a, pltpu.HBM) for a in arrays]


def in_hbm(count):
    return [pl.BlockSpec(memory_space=pltpu.HBM)] * count


def start_copies(pairs, sems):
    copies = [
        pltpu.make_async_copy(source, target, sems.at[k])
        for k, (source, target) in enumerate(pairs)
    ]
    for copy in copies:
        copy.start()
    return copies


def put_pair_weights(target, weights, first, depth, offsets):
    out = weights.shape[2]
    span = depth * len(offsets)
    for a in range(3):
        for place, d in enumerate(offsets):
            rows = pl.ds(a * span + place * depth, depth)
            for q in range(2):
                b = d - q + 1
                lanes = pl.ds(q * out, out)
                if 0 <= b <= 2:
                    target[rows, lanes] = weights[3 * a + b, pl.ds(first, depth), :]
                else:
                    target[rows, lanes] = jnp.zeros((depth, out), target.dtype)


def clear_edges(ref, pairs):
    zero = jnp.zeros((pairs, ref.shape[1]), ref.dtype)
    ref[pl.ds(0, pairs), :] = zero
    ref[pl.ds(ref.shape[0] - pairs, pairs), :] = zero


def pair_taps(taps, weights, start, size, pairs):
    depth = taps.shape[1]
    total = dot(taps[pl.ds(start, size), :], weights[pl.ds(0, depth), :])
    for a in range(1, 3):
        total += dot(
            taps[pl.ds(start + a * pairs, size), :], weights[pl.ds(a * depth, depth), :]
        )
    return total


def column_masks(size, lanes, pairs):
    m = lax.rem(lax.broadcasted_iota(jnp.int32, (size, lanes), 0), pairs)
    return m == 0, m == pairs - 1


def looped(count, body):
    lax.fori_loop(0, count, lambda k, carry: (body(k), carry)[1], 0)


def patches_away(owner_ref):
    return lax.axis_index("patch") ^ owner_ref[lax.axis_index("lead")]


def resident_kernel(
    owner_ref, x_hbm, first_hbm, second_hbm, w_in_hbm, block_hbm,
    acc_ref, proj_ref, flags_ref, block_ref, w_second_hbm, w_glob_hbm,
    x_ref, first_ref, second_ref, in_ref, w_second_ref, w_glob_ref, cells, taps, w_first, w_in, sems,
):
    height, width, channels = x_ref.shape
    pairs = width // 2
    rows = height * pairs
    temporal = in_ref.shape[0]
    glob = first_ref.shape[1] - channels
    parts = 4
    step = height // parts
    slices = [pl.ds(k * step, step) for k in range(parts)]
    copies = start_copies(
        [(x_hbm.at[part, :, :], x_ref.at[part, :, :]) for part in slices]
        + [
            (w_in_hbm, in_ref),
            (first_hbm, first_ref),
            (second_hbm, second_ref),
            (block_hbm.at[pl.ds(0, block_ref.shape[0]), :], block_ref),
        ],
        sems,
    )
    away = patches_away(owner_ref)
    flags_ref[0] = jnp.full(flags_ref.shape[1:], away & 1, jnp.int32)
    flags_ref[1] = jnp.full(flags_ref.shape[1:], away & 2, jnp.int32)
    clear_edges(taps, pairs)
    w_in[...] = jnp.zeros_like(w_in)
    left, right = column_masks(CHUNK, channels, pairs)
    for k in range(parts):
        copies[k].wait()
        for start in range(k * step * pairs, (k + 1) * step * pairs, CHUNK):
            part = x_ref[pl.ds(start // pairs, CHUNK // pairs), :, :].astype(F32)
            cells[pl.ds(EDGE + 2 * start, 2 * CHUNK), :] = part.reshape(2 * CHUNK, channels)
            for place, d in enumerate((-1, 0, 1, 2)):
                value = cells[pl.ds(EDGE + 2 * start + d, CHUNK, stride=2), :]
                if d == -1:
                    value = jnp.where(left, 0.0, value)
                if d == 2:
                    value = jnp.where(right, 0.0, value)
                taps[pl.ds(pairs + start, CHUNK), pl.ds(place * channels, channels)] = value.astype(
                    BF16
                )
    half = rows // 2
    copies[parts].wait()
    for s in range(4):
        w_in[pl.ds(s * temporal, temporal), pl.ds(s * channels, channels)] = in_ref[...]
    for start in range(0, half, CHUNK):
        value = dot_transposed(
            taps[pl.ds(pairs + start, CHUNK), pl.ds(channels, 2 * channels)],
            w_in[:, pl.ds(0, 2 * channels)],
        ) + dot_transposed(
            taps[pl.ds(pairs + half + start, CHUNK), pl.ds(channels, 2 * channels)],
            w_in[:, pl.ds(2 * channels, 2 * channels)],
        )
        proj_ref[pl.ds(start, CHUNK), :] = value.astype(BF16)
    copies[parts + 1].wait()
    put_pair_weights(w_first, first_ref, 0, channels, (-1, 0, 1, 2))
    put_pair_weights(w_glob_ref, first_ref, channels, glob, (0, 1, 2, -1))
    copies[parts + 2].wait()
    put_pair_weights(w_second_ref, second_ref, 0, channels, (-1, 0, 1, 2))
    writes = start_copies(
        [(w_glob_ref, w_glob_hbm), (w_second_ref, w_second_hbm)], sems.at[pl.ds(parts + 4, 2)]
    )
    for start in range(0, rows, WIDE):
        acc_ref[pl.ds(start, WIDE), :] = pair_taps(taps, w_first, start, WIDE, pairs)
    for write in [*writes, copies[parts + 3]]:
        write.wait()


def resident_part(owner, x, w_first, w_second, w_in, block):
    height, width, channels = x.shape
    out = w_first.shape[2]
    temporal = w_in.shape[1]
    w_in = w_in.T
    glob = w_first.shape[1] - channels
    pairs = width // 2
    rows = height * pairs
    results = (
        ((rows, 2 * out), F32),
        ((rows // 2, 4 * temporal), BF16),
        ((2, 1, width * glob), jnp.int32),
        ((height // 2, width * glob), BF16),
        ((12 * out, 2 * out), BF16),
        ((12 * glob, 2 * out), BF16),
    )
    return pl.pallas_call(
        resident_kernel,
        out_shape=tuple(
            space(*kind) for space, kind in zip((pltpu.VMEM,) * 4 + (pltpu.HBM,) * 2, results)
        ),
        in_specs=[pl.BlockSpec(memory_space=pltpu.SMEM)] + in_hbm(5),
        out_specs=tuple(in_vmem(4) + in_hbm(2)),
        scratch_shapes=[
            pltpu.VMEM(x.shape, BF16),
            pltpu.VMEM(w_first.shape, BF16),
            pltpu.VMEM(w_second.shape, BF16),
            pltpu.VMEM(w_in.shape, BF16),
            pltpu.VMEM(*results[4]),
            pltpu.VMEM(*results[5]),
            pltpu.VMEM((2 * rows + 2 * EDGE, channels), F32),
            pltpu.VMEM((rows + 2 * pairs, 4 * channels), BF16),
            pltpu.VMEM((12 * channels, 2 * out), BF16),
            pltpu.VMEM((4 * temporal, 4 * channels), BF16),
            pltpu.SemaphoreType.DMA((10,)),
        ],
        compiler_params=pltpu.CompilerParams(vmem_limit_bytes=VMEM_BYTES),
        cost_estimate=pl.CostEstimate(flops=1024, bytes_accessed=1024, transcendentals=0),
        name="resident_part",
    )(*at_hbm(owner, x, w_first, w_second, w_in, block))


def mix_kernel(
    hours_ref, prev_ref, self_ref, next_ref, mix_ref, out_ref, x_hbm, w_second_hbm, w_glob_hbm,
    lifted_ref, x_ref, w_second_ref, w_glob_ref, w_mix, w_lift, mixed_ref, sems,
):
    copies = start_copies(
        [(w_glob_hbm, w_glob_ref), (w_second_hbm, w_second_ref), (x_hbm, x_ref)], sems
    )
    leads = hours_ref.shape[0]
    temporal = mix_ref.shape[1]
    lead = lax.axis_index("lead")
    now = hours_ref[lead]
    before = hours_ref[jnp.maximum(lead - 1, 0)]
    after = hours_ref[jnp.minimum(lead + 1, leads - 1)]

    def gain(gap, used):
        gap = jnp.full((1, 4 * temporal), gap, jnp.int32).astype(F32)
        return jnp.where(used, jnp.exp(-0.5 * (gap - 1.0)), 0.0)

    gain_prev = gain(now - before, lead > 0)
    gain_next = gain(after - now, lead < leads - 1)
    w_mix[...] = jnp.zeros_like(w_mix)
    for k in range(3):
        for s in range(4):
            w_mix[k, pl.ds(s * temporal, temporal), pl.ds(s * temporal, temporal)] = mix_ref[k]
    rows, out = mixed_ref.shape[0], out_ref.shape[1]
    w_lift[...] = jnp.zeros_like(w_lift)
    for s in range(2):
        for q in range(2):
            w_lift[
                s, pl.ds((2 * s + q) * temporal, temporal), pl.ds(q * out, out)
            ] = out_ref[...]
    for start in range(0, rows, CHUNK):
        part = pl.ds(start, CHUNK)
        value = gain_prev * dot(prev_ref[part, :], w_mix[0])
        value = value + dot(self_ref[part, :], w_mix[1])
        value = value + gain_next * dot(next_ref[part, :], w_mix[2])
        mixed_ref[part, :] = value.astype(BF16)
    for s in range(2):
        lifted_ref[pl.ds(s * rows, rows), :] = dot(mixed_ref[...], w_lift[s])
    for copy in copies:
        copy.wait()


def mix_part(hours, before, own, after, w_mix, w_out, moved):
    lanes, out = own.shape[1], w_out.shape[1]
    return pl.pallas_call(
        mix_kernel,
        out_shape=(
            pltpu.VMEM((2 * own.shape[0], 2 * out), F32),
            *(pltpu.VMEM(a.shape, a.dtype) for a in moved),
        ),
        in_specs=[pl.BlockSpec(memory_space=pltpu.SMEM)] + in_vmem(5) + in_hbm(len(moved)),
        out_specs=tuple(in_vmem(1 + len(moved))),
        scratch_shapes=[
            pltpu.VMEM((3, lanes, lanes), BF16),
            pltpu.VMEM((2, lanes, 2 * out), BF16),
            pltpu.VMEM(own.shape, BF16),
            pltpu.SemaphoreType.DMA((len(moved),)),
        ],
        compiler_params=pltpu.CompilerParams(vmem_limit_bytes=VMEM_BYTES),
        cost_estimate=pl.CostEstimate(
            flops=6 * own.shape[0] * lanes * lanes, bytes_accessed=1024 * 1024, transcendentals=0
        ),
        name="mix_part",
    )(hours, before, own, after, w_mix, w_out, *at_hbm(*moved))


def row_parts(rows, pairs):
    count = max(1, rows * pairs // WIDE)
    bounds = [rows * k // count for k in range(count + 1)]
    return [(low, high - low) for low, high in zip(bounds, bounds[1:])]


def rest_kernel(second, side_of, place, owner_ref, acc_ref, lifted_ref, *refs):
    x_ref, w_second_ref, w_glob_ref, *refs = refs
    middle, refs = refs[:-8], refs[-8:]
    out_ref, glob_cells, glob_taps, odd, even, taps, cells, sems = refs
    if second:
        *pieces, glob_edge, taps_edge, _, out_hbm = middle
    else:
        *pieces, out_hbm, glob_edge, taps_edge = middle
    rows, width, channels = out_ref.shape
    pairs = width // 2
    out = channels
    lanes = glob_cells.shape[1]
    share = pieces[0].shape[0]
    half = share * len(pieces)
    side = side_of(owner_ref)
    first = (1 - side) * (half - 2) if second else side * half
    act_first = (1 - side) * (half - 1) if second else side * half
    act_rows = half + 1 if second else half
    act_place = 2 - side if second else 1
    new_place = 3 - 2 * side if second else 1

    def at(row):
        return pl.multiple_of(row * pairs, pairs)

    clear_edges(glob_taps, pairs)
    clear_edges(taps, pairs)
    for k, piece in enumerate(pieces):
        base = EDGE + at(place(owner_ref, k) * share)
        for m in range(pairs):
            value = piece[:, pl.ds(m * lanes, lanes)].astype(F32)
            glob_cells[pl.ds(base + m, share, stride=pairs), :] = value
    left, right = column_masks(CHUNK, lanes, pairs)
    lower = lax.broadcasted_iota(jnp.int32, (CHUNK, lanes), 1) < lanes // 2
    for start in range(0, half * pairs, CHUNK):
        here = glob_cells[pl.ds(EDGE + start, CHUNK), :]
        before = jnp.where(left, 0.0, glob_cells[pl.ds(EDGE - 1 + start, CHUNK), :])
        after = jnp.where(right, 0.0, glob_cells[pl.ds(EDGE + 1 + start, CHUNK), :])
        part = pl.ds(at(new_place + start // pairs), CHUNK)
        glob_taps[part, pl.ds(0, lanes)] = here.astype(BF16)
        glob_taps[part, pl.ds(lanes, lanes)] = jnp.where(lower, after, before).astype(BF16)
    if second:
        glob_taps[pl.ds(at(1 + half * side), 2 * pairs), :] = glob_edge[...]
        taps[pl.ds(at((half + 2) * side), 2 * pairs), :] = taps_edge[...]
    for low, count in row_parts(act_rows, pairs):
        size = count * pairs
        start = EDGE + low * pairs
        left, right = column_masks(size, out, pairs)
        value = acc_ref[pl.ds(at(act_first + low), size), :] + pair_taps(
            glob_taps, w_glob_ref, at(act_place + low - 1), size, pairs
        )
        value = silu(value)
        even[pl.ds(start, size), :] = value[:, :out]
        odd[pl.ds(start, size), :] = value[:, out:]
        part = pl.ds(at(act_place + low), size)
        taps[part, pl.ds(out, 2 * out)] = value.astype(BF16)
        before = jnp.where(left, 0.0, odd[pl.ds(start - 1, size), :])
        after = jnp.where(right, 0.0, even[pl.ds(start + 1, size), :])
        taps[part, pl.ds(0, out)] = before.astype(BF16)
        taps[part, pl.ds(3 * out, out)] = after.astype(BF16)
    if not second:
        glob_edge[...] = glob_taps[pl.ds(at(1 + (half - 2) * (1 - side)), 2 * pairs), :]
        taps_edge[...] = taps[pl.ds(at(2 + (half - 4) * (1 - side)), 2 * pairs), :]
    writes = []
    for low, count in row_parts(rows, pairs):
        size = count * pairs
        value = pair_taps(taps, w_second_ref, low * pairs, size, pairs)
        value = silu(value + lifted_ref[pl.ds(at(first + low), size), :])
        start = 2 * low * pairs
        cells[pl.ds(start, size, stride=2), :] = value[:, :out]
        cells[pl.ds(start + 1, size, stride=2), :] = value[:, out:]
        for here, count in ((low, count // 2), (low + count // 2, count - count // 2)):
            part = pl.ds(here, count)
            value = cells[pl.ds(here * width, count * width), :].reshape(count, width, channels)
            resident = x_ref[pl.ds(first + here, count), :, :].astype(F32)
            out_ref[part, :, :] = (resident + value).astype(BF16)
            writes += start_copies(
                [(out_ref.at[part, :, :], out_hbm.at[pl.ds(first + here, count), :, :])],
                sems.at[pl.ds(len(writes), 1)],
            )
    for write in writes:
        write.wait()


def rest_part(second, side_of, place, owner, acc, lifted, x, w_second, w_glob, pieces, carried):
    _, width, channels = x.shape
    pairs = width // 2
    lanes = pieces[0].shape[1] // pairs
    half = pieces[0].shape[0] * len(pieces)
    rows = half + 2 if second else half
    space = pltpu.with_memory_space_constraint
    results = (pltpu.HBM(x.shape, BF16),)
    if not second:
        results += (
            pltpu.VMEM((2 * pairs, 2 * lanes), BF16),
            pltpu.VMEM((2 * pairs, 4 * channels), BF16),
        )
    return pl.pallas_call(
        lambda *refs: rest_kernel(second, side_of, place, *refs),
        out_shape=results,
        in_specs=[pl.BlockSpec(memory_space=pltpu.SMEM)]
        + in_vmem(5 + len(pieces))
        + (in_vmem(2) + in_hbm(1) if second else []),
        out_specs=tuple(in_hbm(1) + in_vmem(len(results) - 1)),
        input_output_aliases={8 + len(pieces): 0} if second else {},
        scratch_shapes=[
            pltpu.VMEM((rows, width, channels), BF16),
            pltpu.VMEM((half * pairs + 2 * EDGE, lanes), F32),
            pltpu.VMEM(((rows + 2) * pairs, 2 * lanes), BF16),
            pltpu.VMEM(((half + 1) * pairs + 2 * EDGE, channels), F32),
            pltpu.VMEM(((half + 1) * pairs + 2 * EDGE, channels), F32),
            pltpu.VMEM(((rows + 2) * pairs, 4 * channels), BF16),
            pltpu.VMEM((rows * width, channels), F32),
            pltpu.SemaphoreType.DMA((2 * len(row_parts(rows, pairs)),)),
        ],
        compiler_params=pltpu.CompilerParams(vmem_limit_bytes=VMEM_BYTES),
        cost_estimate=pl.CostEstimate(
            flops=4 * rows * width * 12 * channels * channels,
            bytes_accessed=4 * 1024 * 1024,
            transcendentals=0,
        ),
        name="rest_second" if second else "rest_first",
    )(
        owner,
        *(space(a, pltpu.VMEM) for a in (acc, lifted, x, w_second, w_glob)),
        *pieces,
        *carried,
    )


def rotated(block, axis, distance):
    count = lax.axis_size(axis)
    return lax.ppermute(block, axis, [(i, (i + distance) % count) for i in range(count)])


def swapped(block, bit):
    count = lax.axis_size("patch")
    return lax.ppermute(block, "patch", [(i, i ^ bit) for i in range(count)])


def side_first(owner_ref):
    return patches_away(owner_ref) & 1


def place_first(owner_ref, k):
    return 2 * (k // 2) + (((patches_away(owner_ref) >> 1) ^ k) & 1)


def per_device(
    features, context, owner, hours, w_first, w_second, w_lead_in, w_lead_mix, w_lead_out
):
    resident, block = features[0, 0], context[0, 0]
    acc, proj, flags, kept, w_second, w_glob = resident_part(
        owner, resident, w_first, w_second, w_lead_in, block
    )

    def lifted_with(proj):
        before, after = rotated(proj, "lead", 1), rotated(proj, "lead", -1)
        moved = (resident, w_second, w_glob)
        return mix_part(hours, before, proj, after, w_lead_mix, w_lead_out, moved)

    def rest(second, side_of, place, lifted, pieces, carried):
        return rest_part(second, side_of, place, owner, acc, *lifted, pieces, carried)

    if lax.axis_size("patch") != 4:
        mine = lax.axis_index("patch") == owner[lax.axis_index("lead")]
        whole = lax.psum(jnp.where(mine, block, jnp.zeros_like(block)), "patch")
        result, _, _ = rest(
            False, lambda ref: 0, lambda ref, k: k, lifted_with(proj), [whole], []
        )
        return result[None, None]

    near, beside = flags[0] == 0, flags[1] == 0
    half = block.shape[0] // 2
    share = half // (2 * GROUPS)
    arrived, proj = lax.optimization_barrier((swapped(block[half:], 1), proj))
    owns, acrosses = [], []
    for g in range(GROUPS):
        rows = slice(2 * g * share, 2 * (g + 1) * share)
        part = jnp.where(near, kept[rows], arrived[rows])
        owns += [jnp.where(beside, part[:share], swapped(part[share:], 2))]
        acrosses += [swapped(owns[g], 2)]
    lifted = lifted_with(proj)
    acrosses, lifted = lax.optimization_barrier((acrosses, lifted))
    upper = [piece for pair in zip(owns, acrosses) for piece in pair]
    lower = [swapped(piece, 1) for piece in upper]
    result, *edges = rest(False, side_first, place_first, lifted, upper, [])
    (result,) = rest(True, side_first, place_first, lifted, lower, [*edges, result])
    return result[None, None]


def solution(mesh):
    placed = (
        P(("grp", "lead"), "patch", None, None, None),
        P("patch", ("grp", "lead"), None, None),
        P("grp"),
        P("grp"),
        P(),
        P(),
        P(),
        P(),
        P(),
    )
    return jax.shard_map(
        per_device,
        mesh=mesh,
        in_specs=placed,
        out_specs=P(("grp", "lead"), "patch", None, None, None),
        check_vma=False,
    )
```

```python
import jax
import jax.numpy as jnp
from jax import lax
from jax.experimental import pallas as pl
from jax.experimental.pallas import tpu as pltpu
from jax.sharding import PartitionSpec as P

BF16 = jnp.bfloat16
F32 = jnp.float32
EDGE = 8
CHUNK = 256
WIDE = 1024
GROUPS = 1
VMEM_BYTES = 20 * 1024 * 1024


def silu(v):
    return 0.5 * v * (1.0 + jnp.tanh(0.5 * v))


def dot(a, b):
    return jnp.dot(a, b, preferred_element_type=F32)


def dot_transposed(a, b):
    return lax.dot_general(a, b, (((1,), (1,)), ((), ())), preferred_element_type=F32)


def in_vmem(count):
    return [pl.BlockSpec(memory_space=pltpu.VMEM)] * count


def at_hbm(*arrays):
    return [pltpu.with_memory_space_constraint(a, pltpu.HBM) for a in arrays]


def in_hbm(count):
    return [pl.BlockSpec(memory_space=pltpu.HBM)] * count


def start_copies(pairs, sems):
    copies = [
        pltpu.make_async_copy(source, target, sems.at[k])
        for k, (source, target) in enumerate(pairs)
    ]
    for copy in copies:
        copy.start()
    return copies


def put_pair_weights(target, weights, first, depth, offsets):
    out = weights.shape[2]
    span = depth * len(offsets)
    for a in range(3):
        for place, d in enumerate(offsets):
            rows = pl.ds(a * span + place * depth, depth)
            for q in range(2):
                b = d - q + 1
                lanes = pl.ds(q * out, out)
                if 0 <= b <= 2:
                    target[rows, lanes] = weights[3 * a + b, pl.ds(first, depth), :]
                else:
                    target[rows, lanes] = jnp.zeros((depth, out), target.dtype)


def clear_edges(ref, pairs):
    zero = jnp.zeros((pairs, ref.shape[1]), ref.dtype)
    ref[pl.ds(0, pairs), :] = zero
    ref[pl.ds(ref.shape[0] - pairs, pairs), :] = zero


def pair_taps(taps, weights, start, size, pairs):
    depth = taps.shape[1]
    total = dot(taps[pl.ds(start, size), :], weights[pl.ds(0, depth), :])
    for a in range(1, 3):
        total += dot(
            taps[pl.ds(start + a * pairs, size), :], weights[pl.ds(a * depth, depth), :]
        )
    return total


def column_masks(size, lanes, pairs):
    m = lax.rem(lax.broadcasted_iota(jnp.int32, (size, lanes), 0), pairs)
    return m == 0, m == pairs - 1


def looped(count, body):
    lax.fori_loop(0, count, lambda k, carry: (body(k), carry)[1], 0)


def patches_away(owner_ref):
    return lax.axis_index("patch") ^ owner_ref[lax.axis_index("lead")]


def resident_kernel(
    owner_ref, x_hbm, first_hbm, second_hbm, w_in_hbm, block_hbm,
    acc_ref, proj_ref, flags_ref, block_ref, w_second_ref, w_glob_ref, x_ref,
    first_ref, second_ref, in_ref, cells, taps, w_first, w_in, sems,
):
    height, width, channels = x_ref.shape
    pairs = width // 2
    rows = height * pairs
    temporal = in_ref.shape[0]
    glob = first_ref.shape[1] - channels
    parts = 4
    step = height // parts
    slices = [pl.ds(k * step, step) for k in range(parts)]
    copies = start_copies(
        [(x_hbm.at[part, :, :], x_ref.at[part, :, :]) for part in slices]
        + [
            (w_in_hbm, in_ref),
            (first_hbm, first_ref),
            (second_hbm, second_ref),
            (block_hbm.at[pl.ds(0, block_ref.shape[0]), :], block_ref),
        ],
        sems,
    )
    away = patches_away(owner_ref)
    flags_ref[0] = jnp.full(flags_ref.shape[1:], away & 1, jnp.int32)
    flags_ref[1] = jnp.full(flags_ref.shape[1:], away & 2, jnp.int32)
    clear_edges(taps, pairs)
    w_in[...] = jnp.zeros_like(w_in)
    left, right = column_masks(CHUNK, channels, pairs)
    for k in range(parts):
        copies[k].wait()
        for start in range(k * step * pairs, (k + 1) * step * pairs, CHUNK):
            part = x_ref[pl.ds(start // pairs, CHUNK // pairs), :, :].astype(F32)
            cells[pl.ds(EDGE + 2 * start, 2 * CHUNK), :] = part.reshape(2 * CHUNK, channels)
            for place, d in enumerate((-1, 0, 1, 2)):
                value = cells[pl.ds(EDGE + 2 * start + d, CHUNK, stride=2), :]
                if d == -1:
                    value = jnp.where(left, 0.0, value)
                if d == 2:
                    value = jnp.where(right, 0.0, value)
                taps[pl.ds(pairs + start, CHUNK), pl.ds(place * channels, channels)] = value.astype(
                    BF16
                )
    half = rows // 2
    copies[parts].wait()
    for s in range(4):
        w_in[pl.ds(s * temporal, temporal), pl.ds(s * channels, channels)] = in_ref[...]
    for start in range(0, half, CHUNK):
        value = dot_transposed(
            taps[pl.ds(pairs + start, CHUNK), pl.ds(channels, 2 * channels)],
            w_in[:, pl.ds(0, 2 * channels)],
        ) + dot_transposed(
            taps[pl.ds(pairs + half + start, CHUNK), pl.ds(channels, 2 * channels)],
            w_in[:, pl.ds(2 * channels, 2 * channels)],
        )
        proj_ref[pl.ds(start, CHUNK), :] = value.astype(BF16)
    copies[parts + 1].wait()
    put_pair_weights(w_first, first_ref, 0, channels, (-1, 0, 1, 2))
    put_pair_weights(w_glob_ref, first_ref, channels, glob, (0, 1, 2, -1))
    copies[parts + 2].wait()
    put_pair_weights(w_second_ref, second_ref, 0, channels, (-1, 0, 1, 2))
    for start in range(0, rows, WIDE):
        acc_ref[pl.ds(start, WIDE), :] = pair_taps(taps, w_first, start, WIDE, pairs)
    copies[parts + 3].wait()


def resident_part(owner, x, w_first, w_second, w_in, block):
    height, width, channels = x.shape
    out = w_first.shape[2]
    temporal = w_in.shape[1]
    w_in = w_in.T
    glob = w_first.shape[1] - channels
    pairs = width // 2
    rows = height * pairs
    results = (
        ((rows, 2 * out), F32),
        ((rows // 2, 4 * temporal), BF16),
        ((2, 1, width * glob), jnp.int32),
        ((height // 2, width * glob), BF16),
        ((12 * out, 2 * out), BF16),
        ((12 * glob, 2 * out), BF16),
        (x.shape, BF16),
    )
    return pl.pallas_call(
        resident_kernel,
        out_shape=tuple(
            space(*kind) for space, kind in zip((pltpu.VMEM,) * 7, results)
        ),
        in_specs=[pl.BlockSpec(memory_space=pltpu.SMEM)] + in_hbm(5),
        out_specs=tuple(in_vmem(7)),
        scratch_shapes=[
            pltpu.VMEM(w_first.shape, BF16),
            pltpu.VMEM(w_second.shape, BF16),
            pltpu.VMEM(w_in.shape, BF16),
            pltpu.VMEM((2 * rows + 2 * EDGE, channels), F32),
            pltpu.VMEM((rows + 2 * pairs, 4 * channels), BF16),
            pltpu.VMEM((12 * channels, 2 * out), BF16),
            pltpu.VMEM((4 * temporal, 4 * channels), BF16),
            pltpu.SemaphoreType.DMA((10,)),
        ],
        compiler_params=pltpu.CompilerParams(vmem_limit_bytes=VMEM_BYTES),
        cost_estimate=pl.CostEstimate(flops=1024, bytes_accessed=1024, transcendentals=0),
        name="resident_part",
    )(*at_hbm(owner, x, w_first, w_second, w_in, block))


def mix_kernel(
    hours_ref, prev_ref, self_ref, next_ref, mix_ref, out_ref, lifted_ref, w_mix, w_lift, mixed_ref
):
    leads = hours_ref.shape[0]
    temporal = mix_ref.shape[1]
    lead = lax.axis_index("lead")
    now = hours_ref[lead]
    before = hours_ref[jnp.maximum(lead - 1, 0)]
    after = hours_ref[jnp.minimum(lead + 1, leads - 1)]

    def gain(gap, used):
        gap = jnp.full((1, 4 * temporal), gap, jnp.int32).astype(F32)
        return jnp.where(used, jnp.exp(-0.5 * (gap - 1.0)), 0.0)

    gain_prev = gain(now - before, lead > 0)
    gain_next = gain(after - now, lead < leads - 1)
    w_mix[...] = jnp.zeros_like(w_mix)
    for k in range(3):
        for s in range(4):
            w_mix[k, pl.ds(s * temporal, temporal), pl.ds(s * temporal, temporal)] = mix_ref[k]
    rows, out = mixed_ref.shape[0], out_ref.shape[1]
    w_lift[...] = jnp.zeros_like(w_lift)
    for s in range(2):
        for q in range(2):
            w_lift[
                s, pl.ds((2 * s + q) * temporal, temporal), pl.ds(q * out, out)
            ] = out_ref[...]
    for start in range(0, rows, CHUNK):
        part = pl.ds(start, CHUNK)
        value = gain_prev * dot(prev_ref[part, :], w_mix[0])
        value = value + dot(self_ref[part, :], w_mix[1])
        value = value + gain_next * dot(next_ref[part, :], w_mix[2])
        mixed_ref[part, :] = value.astype(BF16)
    for s in range(2):
        lifted_ref[pl.ds(s * rows, rows), :] = dot(mixed_ref[...], w_lift[s])


def mix_part(hours, before, own, after, w_mix, w_out):
    lanes, out = own.shape[1], w_out.shape[1]
    return pl.pallas_call(
        mix_kernel,
        out_shape=pltpu.VMEM((2 * own.shape[0], 2 * out), F32),
        in_specs=[pl.BlockSpec(memory_space=pltpu.SMEM)] + in_vmem(5),
        out_specs=in_vmem(1)[0],
        scratch_shapes=[
            pltpu.VMEM((3, lanes, lanes), BF16),
            pltpu.VMEM((2, lanes, 2 * out), BF16),
            pltpu.VMEM(own.shape, BF16),
        ],
        compiler_params=pltpu.CompilerParams(vmem_limit_bytes=VMEM_BYTES),
        cost_estimate=pl.CostEstimate(
            flops=6 * own.shape[0] * lanes * lanes, bytes_accessed=1024 * 1024, transcendentals=0
        ),
        name="mix_part",
    )(hours, before, own, after, w_mix, w_out)


def row_parts(rows, pairs):
    count = max(1, rows * pairs // CHUNK)
    bounds = [rows * k // count for k in range(count + 1)]
    return [(low, high - low) for low, high in zip(bounds, bounds[1:])]


def rest_kernel(second, side_of, place, owner_ref, acc_ref, lifted_ref, *refs):
    x_ref, w_second_ref, w_glob_ref, *refs = refs
    middle, refs = refs[:-8], refs[-8:]
    out_ref, glob_cells, glob_taps, odd, even, taps, cells, sems = refs
    if second:
        *pieces, glob_edge, taps_edge, _, out_hbm = middle
    else:
        *pieces, out_hbm, glob_edge, taps_edge = middle
    rows, width, channels = out_ref.shape
    pairs = width // 2
    out = channels
    lanes = glob_cells.shape[1]
    share = pieces[0].shape[0]
    half = share * len(pieces)
    side = side_of(owner_ref)
    first = (1 - side) * (half - 2) if second else side * half
    act_first = (1 - side) * (half - 1) if second else side * half
    act_rows = half + 1 if second else half
    act_place = 2 - side if second else 1
    new_place = 3 - 2 * side if second else 1

    def at(row):
        return pl.multiple_of(row * pairs, pairs)

    clear_edges(glob_taps, pairs)
    clear_edges(taps, pairs)
    for k, piece in enumerate(pieces):
        base = EDGE + at(place(owner_ref, k) * share)
        for m in range(pairs):
            value = piece[:, pl.ds(m * lanes, lanes)].astype(F32)
            glob_cells[pl.ds(base + m, share, stride=pairs), :] = value
    left, right = column_masks(CHUNK, lanes, pairs)
    lower = lax.broadcasted_iota(jnp.int32, (CHUNK, lanes), 1) < lanes // 2
    for start in range(0, half * pairs, CHUNK):
        here = glob_cells[pl.ds(EDGE + start, CHUNK), :]
        before = jnp.where(left, 0.0, glob_cells[pl.ds(EDGE - 1 + start, CHUNK), :])
        after = jnp.where(right, 0.0, glob_cells[pl.ds(EDGE + 1 + start, CHUNK), :])
        part = pl.ds(at(new_place + start // pairs), CHUNK)
        glob_taps[part, pl.ds(0, lanes)] = here.astype(BF16)
        glob_taps[part, pl.ds(lanes, lanes)] = jnp.where(lower, after, before).astype(BF16)
    if second:
        glob_taps[pl.ds(at(1 + half * side), 2 * pairs), :] = glob_edge[...]
        taps[pl.ds(at((half + 2) * side), 2 * pairs), :] = taps_edge[...]
    for low, count in row_parts(act_rows, pairs):
        size = count * pairs
        start = EDGE + low * pairs
        left, right = column_masks(size, out, pairs)
        value = acc_ref[pl.ds(at(act_first + low), size), :] + pair_taps(
            glob_taps, w_glob_ref, at(act_place + low - 1), size, pairs
        )
        value = silu(value)
        even[pl.ds(start, size), :] = value[:, :out]
        odd[pl.ds(start, size), :] = value[:, out:]
        part = pl.ds(at(act_place + low), size)
        taps[part, pl.ds(out, 2 * out)] = value.astype(BF16)
        before = jnp.where(left, 0.0, odd[pl.ds(start - 1, size), :])
        after = jnp.where(right, 0.0, even[pl.ds(start + 1, size), :])
        taps[part, pl.ds(0, out)] = before.astype(BF16)
        taps[part, pl.ds(3 * out, out)] = after.astype(BF16)
    if not second:
        glob_edge[...] = glob_taps[pl.ds(at(1 + (half - 2) * (1 - side)), 2 * pairs), :]
        taps_edge[...] = taps[pl.ds(at(2 + (half - 4) * (1 - side)), 2 * pairs), :]
    writes = []
    for low, count in row_parts(rows, pairs):
        size = count * pairs
        value = pair_taps(taps, w_second_ref, low * pairs, size, pairs)
        value = silu(value + lifted_ref[pl.ds(at(first + low), size), :])
        start = 2 * low * pairs
        cells[pl.ds(start, size, stride=2), :] = value[:, :out]
        cells[pl.ds(start + 1, size, stride=2), :] = value[:, out:]
        for here, count in ((low, count // 2), (low + count // 2, count - count // 2)):
            part = pl.ds(here, count)
            value = cells[pl.ds(here * width, count * width), :].reshape(count, width, channels)
            resident = x_ref[pl.ds(first + here, count), :, :].astype(F32)
            out_ref[part, :, :] = (resident + value).astype(BF16)
            writes += start_copies(
                [(out_ref.at[part, :, :], out_hbm.at[pl.ds(first + here, count), :, :])],
                sems.at[pl.ds(len(writes), 1)],
            )
    for write in writes:
        write.wait()


def rest_part(second, side_of, place, owner, acc, lifted, x, w_second, w_glob, pieces, carried):
    _, width, channels = x.shape
    pairs = width // 2
    lanes = pieces[0].shape[1] // pairs
    half = pieces[0].shape[0] * len(pieces)
    rows = half + 2 if second else half
    space = pltpu.with_memory_space_constraint
    results = (pltpu.HBM(x.shape, BF16),)
    if not second:
        results += (
            pltpu.VMEM((2 * pairs, 2 * lanes), BF16),
            pltpu.VMEM((2 * pairs, 4 * channels), BF16),
        )
    return pl.pallas_call(
        lambda *refs: rest_kernel(second, side_of, place, *refs),
        out_shape=results,
        in_specs=[pl.BlockSpec(memory_space=pltpu.SMEM)]
        + in_vmem(5 + len(pieces))
        + (in_vmem(2) + in_hbm(1) if second else []),
        out_specs=tuple(in_hbm(1) + in_vmem(len(results) - 1)),
        input_output_aliases={8 + len(pieces): 0} if second else {},
        scratch_shapes=[
            pltpu.VMEM((rows, width, channels), BF16),
            pltpu.VMEM((half * pairs + 2 * EDGE, lanes), F32),
            pltpu.VMEM(((rows + 2) * pairs, 2 * lanes), BF16),
            pltpu.VMEM(((half + 1) * pairs + 2 * EDGE, channels), F32),
            pltpu.VMEM(((half + 1) * pairs + 2 * EDGE, channels), F32),
            pltpu.VMEM(((rows + 2) * pairs, 4 * channels), BF16),
            pltpu.VMEM((rows * width, channels), F32),
            pltpu.SemaphoreType.DMA((2 * len(row_parts(rows, pairs)),)),
        ],
        compiler_params=pltpu.CompilerParams(vmem_limit_bytes=VMEM_BYTES),
        cost_estimate=pl.CostEstimate(
            flops=4 * rows * width * 12 * channels * channels,
            bytes_accessed=4 * 1024 * 1024,
            transcendentals=0,
        ),
        name="rest_second" if second else "rest_first",
    )(
        owner,
        *(space(a, pltpu.VMEM) for a in (acc, lifted, x, w_second, w_glob)),
        *pieces,
        *carried,
    )


def rotated(block, axis, distance):
    count = lax.axis_size(axis)
    return lax.ppermute(block, axis, [(i, (i + distance) % count) for i in range(count)])


def swapped(block, bit):
    count = lax.axis_size("patch")
    return lax.ppermute(block, "patch", [(i, i ^ bit) for i in range(count)])


def side_first(owner_ref):
    away = patches_away(owner_ref)
    return (away ^ (away >> 1)) & 1


def place_first(owner_ref, k):
    return 2 * (k // 2) + (((patches_away(owner_ref) >> 1) ^ k) & 1)


def per_device(
    features, context, owner, hours, w_first, w_second, w_lead_in, w_lead_mix, w_lead_out
):
    resident, block = features[0, 0], context[0, 0]
    acc, proj, flags, kept, w_second, w_glob, resident = resident_part(
        owner, resident, w_first, w_second, w_lead_in, block
    )

    def lifted_with(proj):
        before, after = rotated(proj, "lead", 1), rotated(proj, "lead", -1)
        return mix_part(hours, before, proj, after, w_lead_mix, w_lead_out)

    def rest(second, side_of, place, lifted, pieces, carried):
        return rest_part(second, side_of, place, owner, acc, lifted, resident, w_second, w_glob, pieces, carried)

    if lax.axis_size("patch") != 4:
        mine = lax.axis_index("patch") == owner[lax.axis_index("lead")]
        whole = lax.psum(jnp.where(mine, block, jnp.zeros_like(block)), "patch")
        result, _, _ = rest(
            False, lambda ref: 0, lambda ref, k: k, lifted_with(proj), [whole], []
        )
        return result[None, None]

    near, beside = flags[0] == 0, flags[1] == 0
    half = block.shape[0] // 2
    share = half // (2 * GROUPS)
    arrived, proj = lax.optimization_barrier((swapped(block[half:], 1), proj))
    owns, acrosses = [], []
    for g in range(GROUPS):
        rows = slice(2 * g * share, 2 * (g + 1) * share)
        part = jnp.where(near, kept[rows], arrived[rows])
        owns += [jnp.where(beside, part[:share], swapped(part[share:], 3))]
        acrosses += [swapped(owns[g], 3)]
    lifted = lifted_with(proj)
    acrosses, lifted = lax.optimization_barrier((acrosses, lifted))
    upper = [piece for pair in zip(owns, acrosses) for piece in pair]
    lower = [swapped(piece, 1) for piece in upper]
    result, *edges = rest(False, side_first, place_first, lifted, upper, [])
    (result,) = rest(True, side_first, place_first, lifted, lower, [*edges, result])
    return result[None, None]


def solution(mesh):
    placed = (
        P(("grp", "lead"), "patch", None, None, None),
        P("patch", ("grp", "lead"), None, None),
        P("grp"),
        P("grp"),
        P(),
        P(),
        P(),
        P(),
        P(),
    )
    return jax.shard_map(
        per_device,
        mesh=mesh,
        in_specs=placed,
        out_specs=P(("grp", "lead"), "patch", None, None, None),
        check_vma=False,
    )
```

```python
import jax
import jax.numpy as jnp
from jax import lax
from jax.experimental import pallas as pl
from jax.experimental.pallas import tpu as pltpu
from jax.sharding import PartitionSpec as P

BF16 = jnp.bfloat16
F32 = jnp.float32
EDGE = 8
CHUNK = 256
WIDE = 1024
VMEM_BYTES = 20 * 1024 * 1024


def silu(v):
    return 0.5 * v * (1.0 + jnp.tanh(0.5 * v))


def dot(a, b):
    return jnp.dot(a, b, preferred_element_type=F32)


def dot_transposed(a, b):
    return lax.dot_general(a, b, (((1,), (1,)), ((), ())), preferred_element_type=F32)


def in_vmem(count):
    return [pl.BlockSpec(memory_space=pltpu.VMEM)] * count


def at_hbm(*arrays):
    return [pltpu.with_memory_space_constraint(a, pltpu.HBM) for a in arrays]


def in_hbm(count):
    return [pl.BlockSpec(memory_space=pltpu.HBM)] * count


def start_copies(pairs, sems):
    copies = [
        pltpu.make_async_copy(source, target, sems.at[k])
        for k, (source, target) in enumerate(pairs)
    ]
    for copy in copies:
        copy.start()
    return copies


def put_pair_weights(target, weights, first, depth, offsets):
    out = weights.shape[2]
    span = depth * len(offsets)
    for a in range(3):
        for place, d in enumerate(offsets):
            rows = pl.ds(a * span + place * depth, depth)
            for q in range(2):
                b = d - q + 1
                lanes = pl.ds(q * out, out)
                if 0 <= b <= 2:
                    target[rows, lanes] = weights[3 * a + b, pl.ds(first, depth), :]
                else:
                    target[rows, lanes] = jnp.zeros((depth, out), target.dtype)


def clear_edges(ref, pairs):
    zero = jnp.zeros((pairs, ref.shape[1]), ref.dtype)
    ref[pl.ds(0, pairs), :] = zero
    ref[pl.ds(ref.shape[0] - pairs, pairs), :] = zero


def pair_taps(taps, weights, start, size, pairs):
    depth = taps.shape[1]
    total = dot(taps[pl.ds(start, size), :], weights[pl.ds(0, depth), :])
    for a in range(1, 3):
        total += dot(
            taps[pl.ds(start + a * pairs, size), :], weights[pl.ds(a * depth, depth), :]
        )
    return total


def column_masks(size, lanes, pairs):
    m = lax.rem(lax.broadcasted_iota(jnp.int32, (size, lanes), 0), pairs)
    return m == 0, m == pairs - 1


def looped(count, body):
    lax.fori_loop(0, count, lambda k, carry: (body(k), carry)[1], 0)


def patches_away(owner_ref):
    return lax.axis_index("patch") ^ owner_ref[lax.axis_index("lead")]


def resident_kernel(
    owner_ref, x_hbm, first_hbm, second_hbm, w_in_hbm, block_hbm,
    acc_ref, proj_ref, flags_ref, block_ref, w_second_ref, w_glob_ref, x_ref,
    first_ref, second_ref, in_ref, cells, taps, w_first, w_in, sems,
):
    height, width, channels = x_ref.shape
    pairs = width // 2
    rows = height * pairs
    temporal = in_ref.shape[0]
    glob = first_ref.shape[1] - channels
    parts = 4
    step = height // parts
    slices = [pl.ds(k * step, step) for k in range(parts)]
    copies = start_copies(
        [(x_hbm.at[part, :, :], x_ref.at[part, :, :]) for part in slices]
        + [
            (w_in_hbm, in_ref),
            (first_hbm, first_ref),
            (second_hbm, second_ref),
            (block_hbm.at[pl.ds(0, block_ref.shape[0]), :], block_ref),
        ],
        sems,
    )
    away = patches_away(owner_ref)
    flags_ref[0] = jnp.full(flags_ref.shape[1:], away & 1, jnp.int32)
    flags_ref[1] = jnp.full(flags_ref.shape[1:], away & 2, jnp.int32)
    clear_edges(taps, pairs)
    w_in[...] = jnp.zeros_like(w_in)
    left, right = column_masks(CHUNK, channels, pairs)
    for k in range(parts):
        copies[k].wait()
        for start in range(k * step * pairs, (k + 1) * step * pairs, CHUNK):
            part = x_ref[pl.ds(start // pairs, CHUNK // pairs), :, :].astype(F32)
            cells[pl.ds(EDGE + 2 * start, 2 * CHUNK), :] = part.reshape(2 * CHUNK, channels)
            for place, d in enumerate((-1, 0, 1, 2)):
                value = cells[pl.ds(EDGE + 2 * start + d, CHUNK, stride=2), :]
                if d == -1:
                    value = jnp.where(left, 0.0, value)
                if d == 2:
                    value = jnp.where(right, 0.0, value)
                taps[pl.ds(pairs + start, CHUNK), pl.ds(place * channels, channels)] = value.astype(
                    BF16
                )
    half = rows // 2
    copies[parts].wait()
    for s in range(4):
        w_in[pl.ds(s * temporal, temporal), pl.ds(s * channels, channels)] = in_ref[...]
    for start in range(0, half, CHUNK):
        value = dot_transposed(
            taps[pl.ds(pairs + start, CHUNK), pl.ds(channels, 2 * channels)],
            w_in[:, pl.ds(0, 2 * channels)],
        ) + dot_transposed(
            taps[pl.ds(pairs + half + start, CHUNK), pl.ds(channels, 2 * channels)],
            w_in[:, pl.ds(2 * channels, 2 * channels)],
        )
        proj_ref[pl.ds(start, CHUNK), :] = value.astype(BF16)
    copies[parts + 1].wait()
    put_pair_weights(w_first, first_ref, 0, channels, (-1, 0, 1, 2))
    put_pair_weights(w_glob_ref, first_ref, channels, glob, (0, 1, 2, -1))
    copies[parts + 2].wait()
    put_pair_weights(w_second_ref, second_ref, 0, channels, (-1, 0, 1, 2))
    for start in range(0, rows, WIDE):
        acc_ref[pl.ds(start, WIDE), :] = pair_taps(taps, w_first, start, WIDE, pairs)
    copies[parts + 3].wait()


def resident_part(owner, x, w_first, w_second, w_in, block):
    height, width, channels = x.shape
    out = w_first.shape[2]
    temporal = w_in.shape[1]
    w_in = w_in.T
    glob = w_first.shape[1] - channels
    pairs = width // 2
    rows = height * pairs
    results = (
        ((rows, 2 * out), F32),
        ((rows // 2, 4 * temporal), BF16),
        ((2, 1, width * glob), jnp.int32),
        ((height // 2, width * glob), BF16),
        ((12 * out, 2 * out), BF16),
        ((12 * glob, 2 * out), BF16),
        (x.shape, BF16),
    )
    return pl.pallas_call(
        resident_kernel,
        out_shape=tuple(
            space(*kind) for space, kind in zip((pltpu.VMEM,) * 7, results)
        ),
        in_specs=[pl.BlockSpec(memory_space=pltpu.SMEM)] + in_hbm(5),
        out_specs=tuple(in_vmem(7)),
        scratch_shapes=[
            pltpu.VMEM(w_first.shape, BF16),
            pltpu.VMEM(w_second.shape, BF16),
            pltpu.VMEM(w_in.shape, BF16),
            pltpu.VMEM((2 * rows + 2 * EDGE, channels), F32),
            pltpu.VMEM((rows + 2 * pairs, 4 * channels), BF16),
            pltpu.VMEM((12 * channels, 2 * out), BF16),
            pltpu.VMEM((4 * temporal, 4 * channels), BF16),
            pltpu.SemaphoreType.DMA((10,)),
        ],
        compiler_params=pltpu.CompilerParams(vmem_limit_bytes=VMEM_BYTES),
        cost_estimate=pl.CostEstimate(flops=1024, bytes_accessed=1024, transcendentals=0),
        name="resident_part",
    )(*at_hbm(owner, x, w_first, w_second, w_in, block))


def mix_kernel(
    hours_ref, prev_ref, self_ref, next_ref, mix_ref, out_ref, lifted_ref, w_mix, w_lift, mixed_ref
):
    leads = hours_ref.shape[0]
    temporal = mix_ref.shape[1]
    lead = lax.axis_index("lead")
    now = hours_ref[lead]
    before = hours_ref[jnp.maximum(lead - 1, 0)]
    after = hours_ref[jnp.minimum(lead + 1, leads - 1)]

    def gain(gap, used):
        gap = jnp.full((1, 4 * temporal), gap, jnp.int32).astype(F32)
        return jnp.where(used, jnp.exp(-0.5 * (gap - 1.0)), 0.0)

    gain_prev = gain(now - before, lead > 0)
    gain_next = gain(after - now, lead < leads - 1)
    w_mix[...] = jnp.zeros_like(w_mix)
    for k in range(3):
        for s in range(4):
            w_mix[k, pl.ds(s * temporal, temporal), pl.ds(s * temporal, temporal)] = mix_ref[k]
    rows, out = mixed_ref.shape[0], out_ref.shape[1]
    w_lift[...] = jnp.zeros_like(w_lift)
    for s in range(2):
        for q in range(2):
            w_lift[
                s, pl.ds((2 * s + q) * temporal, temporal), pl.ds(q * out, out)
            ] = out_ref[...]
    for start in range(0, rows, CHUNK):
        part = pl.ds(start, CHUNK)
        value = gain_prev * dot(prev_ref[part, :], w_mix[0])
        value = value + dot(self_ref[part, :], w_mix[1])
        value = value + gain_next * dot(next_ref[part, :], w_mix[2])
        mixed_ref[part, :] = value.astype(BF16)
    for s in range(2):
        lifted_ref[pl.ds(s * rows, rows), :] = dot(mixed_ref[...], w_lift[s])


def mix_part(hours, before, own, after, w_mix, w_out):
    lanes, out = own.shape[1], w_out.shape[1]
    return pl.pallas_call(
        mix_kernel,
        out_shape=pltpu.VMEM((2 * own.shape[0], 2 * out), F32),
        in_specs=[pl.BlockSpec(memory_space=pltpu.SMEM)] + in_vmem(5),
        out_specs=in_vmem(1)[0],
        scratch_shapes=[
            pltpu.VMEM((3, lanes, lanes), BF16),
            pltpu.VMEM((2, lanes, 2 * out), BF16),
            pltpu.VMEM(own.shape, BF16),
        ],
        compiler_params=pltpu.CompilerParams(vmem_limit_bytes=VMEM_BYTES),
        cost_estimate=pl.CostEstimate(
            flops=6 * own.shape[0] * lanes * lanes, bytes_accessed=1024 * 1024, transcendentals=0
        ),
        name="mix_part",
    )(hours, before, own, after, w_mix, w_out)


def row_parts(rows, pairs):
    count = max(1, rows * pairs // CHUNK)
    bounds = [rows * k // count for k in range(count + 1)]
    return [(low, high - low) for low, high in zip(bounds, bounds[1:])]


def rest_kernel(second, side_of, place, owner_ref, acc_ref, lifted_ref, *refs):
    x_ref, w_second_ref, w_glob_ref, *refs = refs
    middle, refs = refs[:-8], refs[-8:]
    out_ref, glob_cells, glob_taps, odd, even, taps, cells, sems = refs
    if second:
        *pieces, glob_edge, taps_edge, _, out_hbm = middle
    else:
        *pieces, out_hbm, glob_edge, taps_edge = middle
    rows, width, channels = out_ref.shape
    pairs = width // 2
    out = channels
    lanes = glob_cells.shape[1]
    share = pieces[0].shape[0]
    half = share * len(pieces)
    side = side_of(owner_ref)
    first = (1 - side) * (half - 2) if second else side * half
    act_first = (1 - side) * (half - 1) if second else side * half
    act_rows = half + 1 if second else half
    act_place = 2 - side if second else 1
    new_place = 3 - 2 * side if second else 1

    def at(row):
        return pl.multiple_of(row * pairs, pairs)

    clear_edges(glob_taps, pairs)
    clear_edges(taps, pairs)
    for k, piece in enumerate(pieces):
        base = EDGE + at(place(owner_ref, k) * share)
        for m in range(pairs):
            value = piece[:, pl.ds(m * lanes, lanes)].astype(F32)
            glob_cells[pl.ds(base + m, share, stride=pairs), :] = value
    left, right = column_masks(CHUNK, lanes, pairs)
    lower = lax.broadcasted_iota(jnp.int32, (CHUNK, lanes), 1) < lanes // 2
    for start in range(0, half * pairs, CHUNK):
        here = glob_cells[pl.ds(EDGE + start, CHUNK), :]
        before = jnp.where(left, 0.0, glob_cells[pl.ds(EDGE - 1 + start, CHUNK), :])
        after = jnp.where(right, 0.0, glob_cells[pl.ds(EDGE + 1 + start, CHUNK), :])
        part = pl.ds(at(new_place + start // pairs), CHUNK)
        glob_taps[part, pl.ds(0, lanes)] = here.astype(BF16)
        glob_taps[part, pl.ds(lanes, lanes)] = jnp.where(lower, after, before).astype(BF16)
    if second:
        glob_taps[pl.ds(at(1 + half * side), 2 * pairs), :] = glob_edge[...]
        taps[pl.ds(at((half + 2) * side), 2 * pairs), :] = taps_edge[...]
    for low, count in row_parts(act_rows, pairs):
        size = count * pairs
        start = EDGE + low * pairs
        left, right = column_masks(size, out, pairs)
        value = acc_ref[pl.ds(at(act_first + low), size), :] + pair_taps(
            glob_taps, w_glob_ref, at(act_place + low - 1), size, pairs
        )
        value = silu(value)
        even[pl.ds(start, size), :] = value[:, :out]
        odd[pl.ds(start, size), :] = value[:, out:]
        part = pl.ds(at(act_place + low), size)
        taps[part, pl.ds(out, 2 * out)] = value.astype(BF16)
        before = jnp.where(left, 0.0, odd[pl.ds(start - 1, size), :])
        after = jnp.where(right, 0.0, even[pl.ds(start + 1, size), :])
        taps[part, pl.ds(0, out)] = before.astype(BF16)
        taps[part, pl.ds(3 * out, out)] = after.astype(BF16)
    if not second:
        glob_edge[...] = glob_taps[pl.ds(at(1 + (half - 2) * (1 - side)), 2 * pairs), :]
        taps_edge[...] = taps[pl.ds(at(2 + (half - 4) * (1 - side)), 2 * pairs), :]
    writes = []
    for low, count in row_parts(rows, pairs):
        size = count * pairs
        value = pair_taps(taps, w_second_ref, low * pairs, size, pairs)
        value = silu(value + lifted_ref[pl.ds(at(first + low), size), :])
        start = 2 * low * pairs
        cells[pl.ds(start, size, stride=2), :] = value[:, :out]
        cells[pl.ds(start + 1, size, stride=2), :] = value[:, out:]
        for here, count in ((low, count // 2), (low + count // 2, count - count // 2)):
            part = pl.ds(here, count)
            value = cells[pl.ds(here * width, count * width), :].reshape(count, width, channels)
            resident = x_ref[pl.ds(first + here, count), :, :].astype(F32)
            out_ref[part, :, :] = (resident + value).astype(BF16)
            writes += start_copies(
                [(out_ref.at[part, :, :], out_hbm.at[pl.ds(first + here, count), :, :])],
                sems.at[pl.ds(len(writes), 1)],
            )
    for write in writes:
        write.wait()


def rest_part(second, side_of, place, owner, acc, lifted, x, w_second, w_glob, pieces, carried):
    _, width, channels = x.shape
    pairs = width // 2
    lanes = pieces[0].shape[1] // pairs
    half = pieces[0].shape[0] * len(pieces)
    rows = half + 2 if second else half
    space = pltpu.with_memory_space_constraint
    results = (pltpu.HBM(x.shape, BF16),)
    if not second:
        results += (
            pltpu.VMEM((2 * pairs, 2 * lanes), BF16),
            pltpu.VMEM((2 * pairs, 4 * channels), BF16),
        )
    return pl.pallas_call(
        lambda *refs: rest_kernel(second, side_of, place, *refs),
        out_shape=results,
        in_specs=[pl.BlockSpec(memory_space=pltpu.SMEM)]
        + in_vmem(5 + len(pieces))
        + (in_vmem(2) + in_hbm(1) if second else []),
        out_specs=tuple(in_hbm(1) + in_vmem(len(results) - 1)),
        input_output_aliases={8 + len(pieces): 0} if second else {},
        scratch_shapes=[
            pltpu.VMEM((rows, width, channels), BF16),
            pltpu.VMEM((half * pairs + 2 * EDGE, lanes), F32),
            pltpu.VMEM(((rows + 2) * pairs, 2 * lanes), BF16),
            pltpu.VMEM(((half + 1) * pairs + 2 * EDGE, channels), F32),
            pltpu.VMEM(((half + 1) * pairs + 2 * EDGE, channels), F32),
            pltpu.VMEM(((rows + 2) * pairs, 4 * channels), BF16),
            pltpu.VMEM((rows * width, channels), F32),
            pltpu.SemaphoreType.DMA((2 * len(row_parts(rows, pairs)),)),
        ],
        compiler_params=pltpu.CompilerParams(vmem_limit_bytes=VMEM_BYTES),
        cost_estimate=pl.CostEstimate(
            flops=4 * rows * width * 12 * channels * channels,
            bytes_accessed=4 * 1024 * 1024,
            transcendentals=0,
        ),
        name="rest_second" if second else "rest_first",
    )(
        owner,
        *(space(a, pltpu.VMEM) for a in (acc, lifted, x, w_second, w_glob)),
        *pieces,
        *carried,
    )


def rotated(block, axis, distance):
    count = lax.axis_size(axis)
    return lax.ppermute(block, axis, [(i, (i + distance) % count) for i in range(count)])


def swapped(block, bit):
    count = lax.axis_size("patch")
    return lax.ppermute(block, "patch", [(i, i ^ bit) for i in range(count)])


def side_first(owner_ref):
    away = patches_away(owner_ref)
    return (away ^ (away >> 1)) & 1


def place_first(owner_ref, k):
    return ((patches_away(owner_ref) >> 1) ^ k) & 1


def per_device(
    features, context, owner, hours, w_first, w_second, w_lead_in, w_lead_mix, w_lead_out
):
    resident, block = features[0, 0], context[0, 0]
    acc, proj, flags, kept, w_second, w_glob, resident = resident_part(
        owner, resident, w_first, w_second, w_lead_in, block
    )

    def lifted_with(proj):
        before, after = rotated(proj, "lead", 1), rotated(proj, "lead", -1)
        return mix_part(hours, before, proj, after, w_lead_mix, w_lead_out)

    def rest(second, side_of, place, lifted, pieces, carried):
        return rest_part(second, side_of, place, owner, acc, lifted, resident, w_second, w_glob, pieces, carried)

    if lax.axis_size("patch") != 4:
        mine = lax.axis_index("patch") == owner[lax.axis_index("lead")]
        whole = lax.psum(jnp.where(mine, block, jnp.zeros_like(block)), "patch")
        result, _, _ = rest(
            False, lambda ref: 0, lambda ref, k: k, lifted_with(proj), [whole], []
        )
        return result[None, None]

    near, beside = flags[0] == 0, flags[1] == 0
    half = block.shape[0] // 2
    share = half // 2
    passing = swapped(block[half + share :], 1)
    staying = swapped(block[half : half + share], 1)
    passing, proj = lax.optimization_barrier((passing, proj))
    passing = jnp.where(near, kept[share:], passing)
    staying = jnp.where(near, kept[:share], staying)
    own = jnp.where(beside, staying, swapped(passing, 3))
    across = swapped(own, 3)
    lifted = lifted_with(proj)
    across, lifted = lax.optimization_barrier((across, lifted))
    upper = [own, across]
    lower = [swapped(own, 1), swapped(across, 1)]
    result, *edges = rest(False, side_first, place_first, lifted, upper, [])
    (result,) = rest(True, side_first, place_first, lifted, lower, [*edges, result])
    return result[None, None]


def solution(mesh):
    placed = (
        P(("grp", "lead"), "patch", None, None, None),
        P("patch", ("grp", "lead"), None, None),
        P("grp"),
        P("grp"),
        P(),
        P(),
        P(),
        P(),
        P(),
    )
    return jax.shard_map(
        per_device,
        mesh=mesh,
        in_specs=placed,
        out_specs=P(("grp", "lead"), "patch", None, None, None),
        check_vma=False,
    )
```

```python
import jax
import jax.numpy as jnp
from jax import lax
from jax.experimental import pallas as pl
from jax.experimental.pallas import tpu as pltpu
from jax.sharding import PartitionSpec as P

BF16 = jnp.bfloat16
F32 = jnp.float32
EDGE = 8
CHUNK = 256
WIDE = 1024
VMEM_BYTES = 20 * 1024 * 1024


def silu(v):
    return 0.5 * v * (1.0 + jnp.tanh(0.5 * v))


def dot(a, b):
    return jnp.dot(a, b, preferred_element_type=F32)


def dot_transposed(a, b):
    return lax.dot_general(a, b, (((1,), (1,)), ((), ())), preferred_element_type=F32)


def in_vmem(count):
    return [pl.BlockSpec(memory_space=pltpu.VMEM)] * count


def at_hbm(*arrays):
    return [pltpu.with_memory_space_constraint(a, pltpu.HBM) for a in arrays]


def in_hbm(count):
    return [pl.BlockSpec(memory_space=pltpu.HBM)] * count


def start_copies(pairs, sems):
    copies = [
        pltpu.make_async_copy(source, target, sems.at[k])
        for k, (source, target) in enumerate(pairs)
    ]
    for copy in copies:
        copy.start()
    return copies


def put_pair_weights(target, weights, first, depth, offsets):
    out = weights.shape[2]
    span = depth * len(offsets)
    for a in range(3):
        for place, d in enumerate(offsets):
            rows = pl.ds(a * span + place * depth, depth)
            for q in range(2):
                b = d - q + 1
                lanes = pl.ds(q * out, out)
                if 0 <= b <= 2:
                    target[rows, lanes] = weights[3 * a + b, pl.ds(first, depth), :]
                else:
                    target[rows, lanes] = jnp.zeros((depth, out), target.dtype)


def clear_edges(ref, pairs):
    zero = jnp.zeros((pairs, ref.shape[1]), ref.dtype)
    ref[pl.ds(0, pairs), :] = zero
    ref[pl.ds(ref.shape[0] - pairs, pairs), :] = zero


def pair_taps(taps, weights, start, size, pairs):
    depth = taps.shape[1]
    total = dot(taps[pl.ds(start, size), :], weights[pl.ds(0, depth), :])
    for a in range(1, 3):
        total += dot(
            taps[pl.ds(start + a * pairs, size), :], weights[pl.ds(a * depth, depth), :]
        )
    return total


def column_masks(size, lanes, pairs):
    m = lax.rem(lax.broadcasted_iota(jnp.int32, (size, lanes), 0), pairs)
    return m == 0, m == pairs - 1


def looped(count, body):
    lax.fori_loop(0, count, lambda k, carry: (body(k), carry)[1], 0)


def patches_away(owner_ref):
    return lax.axis_index("patch") ^ owner_ref[lax.axis_index("lead")]


def resident_kernel(
    owner_hbm, x_hbm, first_hbm, second_hbm, w_in_hbm, block_hbm,
    acc_ref, proj_ref, flags_ref, block_ref, w_second_ref, w_glob_ref, x_ref,
    first_ref, second_ref, in_ref, owner_ref, cells, taps, w_first, w_in, sems,
):
    height, width, channels = x_ref.shape
    pairs = width // 2
    rows = height * pairs
    temporal = in_ref.shape[0]
    glob = first_ref.shape[1] - channels
    parts = 4
    step = height // parts
    slices = [pl.ds(k * step, step) for k in range(parts)]
    copies = start_copies(
        [(x_hbm.at[part, :, :], x_ref.at[part, :, :]) for part in slices]
        + [
            (w_in_hbm, in_ref),
            (first_hbm, first_ref),
            (second_hbm, second_ref),
            (block_hbm.at[pl.ds(0, block_ref.shape[0]), :], block_ref),
            (owner_hbm, owner_ref),
        ],
        sems,
    )
    clear_edges(taps, pairs)
    w_in[...] = jnp.zeros_like(w_in)
    left, right = column_masks(CHUNK, channels, pairs)
    for k in range(parts):
        copies[k].wait()
        for start in range(k * step * pairs, (k + 1) * step * pairs, CHUNK):
            part = x_ref[pl.ds(start // pairs, CHUNK // pairs), :, :].astype(F32)
            cells[pl.ds(EDGE + 2 * start, 2 * CHUNK), :] = part.reshape(2 * CHUNK, channels)
            for place, d in enumerate((-1, 0, 1, 2)):
                value = cells[pl.ds(EDGE + 2 * start + d, CHUNK, stride=2), :]
                if d == -1:
                    value = jnp.where(left, 0.0, value)
                if d == 2:
                    value = jnp.where(right, 0.0, value)
                taps[pl.ds(pairs + start, CHUNK), pl.ds(place * channels, channels)] = value.astype(
                    BF16
                )
    half = rows // 2
    copies[parts].wait()
    for s in range(4):
        w_in[pl.ds(s * temporal, temporal), pl.ds(s * channels, channels)] = in_ref[...]
    for start in range(0, half, CHUNK):
        value = dot_transposed(
            taps[pl.ds(pairs + start, CHUNK), pl.ds(channels, 2 * channels)],
            w_in[:, pl.ds(0, 2 * channels)],
        ) + dot_transposed(
            taps[pl.ds(pairs + half + start, CHUNK), pl.ds(channels, 2 * channels)],
            w_in[:, pl.ds(2 * channels, 2 * channels)],
        )
        proj_ref[pl.ds(start, CHUNK), :] = value.astype(BF16)
    copies[parts + 1].wait()
    put_pair_weights(w_first, first_ref, 0, channels, (-1, 0, 1, 2))
    put_pair_weights(w_glob_ref, first_ref, channels, glob, (0, 1, 2, -1))
    copies[parts + 2].wait()
    put_pair_weights(w_second_ref, second_ref, 0, channels, (-1, 0, 1, 2))
    for start in range(0, rows, WIDE):
        acc_ref[pl.ds(start, WIDE), :] = pair_taps(taps, w_first, start, WIDE, pairs)
    copies[parts + 3].wait()
    copies[parts + 4].wait()
    away = patches_away(owner_ref)
    flags_ref[0] = jnp.full(flags_ref.shape[1:], away & 1, jnp.int32)
    flags_ref[1] = jnp.full(flags_ref.shape[1:], away & 2, jnp.int32)


def resident_part(owner, x, w_first, w_second, w_in, block):
    height, width, channels = x.shape
    out = w_first.shape[2]
    temporal = w_in.shape[1]
    w_in = w_in.T
    glob = w_first.shape[1] - channels
    pairs = width // 2
    rows = height * pairs
    results = (
        ((rows, 2 * out), F32),
        ((rows // 2, 4 * temporal), BF16),
        ((2, 1, width * glob), jnp.int32),
        ((height // 2, width * glob), BF16),
        ((12 * out, 2 * out), BF16),
        ((12 * glob, 2 * out), BF16),
        (x.shape, BF16),
    )
    return pl.pallas_call(
        resident_kernel,
        out_shape=tuple(
            space(*kind) for space, kind in zip((pltpu.VMEM,) * 7, results)
        ),
        in_specs=in_hbm(6),
        out_specs=tuple(in_vmem(7)),
        scratch_shapes=[
            pltpu.VMEM(w_first.shape, BF16),
            pltpu.VMEM(w_second.shape, BF16),
            pltpu.VMEM(w_in.shape, BF16),
            pltpu.SMEM(owner.shape, jnp.int32),
            pltpu.VMEM((2 * rows + 2 * EDGE, channels), F32),
            pltpu.VMEM((rows + 2 * pairs, 4 * channels), BF16),
            pltpu.VMEM((12 * channels, 2 * out), BF16),
            pltpu.VMEM((4 * temporal, 4 * channels), BF16),
            pltpu.SemaphoreType.DMA((9,)),
        ],
        compiler_params=pltpu.CompilerParams(vmem_limit_bytes=VMEM_BYTES),
        cost_estimate=pl.CostEstimate(flops=1024, bytes_accessed=1024, transcendentals=0),
        name="resident_part",
    )(*at_hbm(owner, x, w_first, w_second, w_in, block))


def mix_kernel(
    hours_hbm, prev_ref, self_ref, next_ref, mix_ref, out_ref, lifted_ref,
    w_mix, w_lift, mixed_ref, hours_ref, sem,
):
    hours_copy = pltpu.make_async_copy(hours_hbm, hours_ref, sem)
    hours_copy.start()
    temporal = mix_ref.shape[1]
    w_mix[...] = jnp.zeros_like(w_mix)
    for k in range(3):
        for s in range(4):
            w_mix[k, pl.ds(s * temporal, temporal), pl.ds(s * temporal, temporal)] = mix_ref[k]
    rows, out = mixed_ref.shape[0], out_ref.shape[1]
    w_lift[...] = jnp.zeros_like(w_lift)
    for s in range(2):
        for q in range(2):
            w_lift[
                s, pl.ds((2 * s + q) * temporal, temporal), pl.ds(q * out, out)
            ] = out_ref[...]
    hours_copy.wait()
    leads = hours_ref.shape[0]
    lead = lax.axis_index("lead")
    now = hours_ref[lead]
    before = hours_ref[jnp.maximum(lead - 1, 0)]
    after = hours_ref[jnp.minimum(lead + 1, leads - 1)]

    def gain(gap, used):
        gap = jnp.full((1, 4 * temporal), gap, jnp.int32).astype(F32)
        return jnp.where(used, jnp.exp(-0.5 * (gap - 1.0)), 0.0)

    gain_prev = gain(now - before, lead > 0)
    gain_next = gain(after - now, lead < leads - 1)
    for start in range(0, rows, CHUNK):
        part = pl.ds(start, CHUNK)
        value = gain_prev * dot(prev_ref[part, :], w_mix[0])
        value = value + dot(self_ref[part, :], w_mix[1])
        value = value + gain_next * dot(next_ref[part, :], w_mix[2])
        mixed_ref[part, :] = value.astype(BF16)
    for s in range(2):
        lifted_ref[pl.ds(s * rows, rows), :] = dot(mixed_ref[...], w_lift[s])


def mix_part(hours, before, own, after, w_mix, w_out):
    lanes, out = own.shape[1], w_out.shape[1]
    return pl.pallas_call(
        mix_kernel,
        out_shape=pltpu.VMEM((2 * own.shape[0], 2 * out), F32),
        in_specs=in_hbm(1) + in_vmem(5),
        out_specs=in_vmem(1)[0],
        scratch_shapes=[
            pltpu.VMEM((3, lanes, lanes), BF16),
            pltpu.VMEM((2, lanes, 2 * out), BF16),
            pltpu.VMEM(own.shape, BF16),
            pltpu.SMEM(hours.shape, jnp.int32),
            pltpu.SemaphoreType.DMA(()),
        ],
        compiler_params=pltpu.CompilerParams(vmem_limit_bytes=VMEM_BYTES),
        cost_estimate=pl.CostEstimate(
            flops=6 * own.shape[0] * lanes * lanes, bytes_accessed=1024 * 1024, transcendentals=0
        ),
        name="mix_part",
    )(*at_hbm(hours), before, own, after, w_mix, w_out)


def row_parts(rows, pairs):
    count = max(1, rows * pairs // CHUNK)
    bounds = [rows * k // count for k in range(count + 1)]
    return [(low, high - low) for low, high in zip(bounds, bounds[1:])]


def rest_kernel(second, side_of, place, flags_ref, acc_ref, lifted_ref, *refs):
    x_ref, w_second_ref, w_glob_ref, *refs = refs
    middle, refs = refs[:-8], refs[-8:]
    out_ref, glob_cells, glob_taps, odd, even, taps, cells, sems = refs
    if second:
        *pieces, glob_edge, taps_edge, _, out_hbm = middle
    else:
        *pieces, out_hbm, glob_edge, taps_edge = middle
    rows, width, channels = out_ref.shape
    pairs = width // 2
    out = channels
    lanes = glob_cells.shape[1]
    share = pieces[0].shape[0]
    half = share * len(pieces)
    away = jnp.max(flags_ref[0, :, :128]) + jnp.max(flags_ref[1, :, :128])
    side = side_of(away)
    first = (1 - side) * (half - 2) if second else side * half
    act_first = (1 - side) * (half - 1) if second else side * half
    act_rows = half + 1 if second else half
    act_place = 2 - side if second else 1
    new_place = 3 - 2 * side if second else 1

    def at(row):
        return pl.multiple_of(row * pairs, pairs)

    clear_edges(glob_taps, pairs)
    clear_edges(taps, pairs)
    for k, piece in enumerate(pieces):
        base = EDGE + at(place(away, k) * share)
        for m in range(pairs):
            value = piece[:, pl.ds(m * lanes, lanes)].astype(F32)
            glob_cells[pl.ds(base + m, share, stride=pairs), :] = value
    left, right = column_masks(CHUNK, lanes, pairs)
    lower = lax.broadcasted_iota(jnp.int32, (CHUNK, lanes), 1) < lanes // 2
    for start in range(0, half * pairs, CHUNK):
        here = glob_cells[pl.ds(EDGE + start, CHUNK), :]
        before = jnp.where(left, 0.0, glob_cells[pl.ds(EDGE - 1 + start, CHUNK), :])
        after = jnp.where(right, 0.0, glob_cells[pl.ds(EDGE + 1 + start, CHUNK), :])
        part = pl.ds(at(new_place + start // pairs), CHUNK)
        glob_taps[part, pl.ds(0, lanes)] = here.astype(BF16)
        glob_taps[part, pl.ds(lanes, lanes)] = jnp.where(lower, after, before).astype(BF16)
    if second:
        glob_taps[pl.ds(at(1 + half * side), 2 * pairs), :] = glob_edge[...]
        taps[pl.ds(at((half + 2) * side), 2 * pairs), :] = taps_edge[...]
    for low, count in row_parts(act_rows, pairs):
        size = count * pairs
        start = EDGE + low * pairs
        left, right = column_masks(size, out, pairs)
        value = acc_ref[pl.ds(at(act_first + low), size), :] + pair_taps(
            glob_taps, w_glob_ref, at(act_place + low - 1), size, pairs
        )
        value = silu(value)
        even[pl.ds(start, size), :] = value[:, :out]
        odd[pl.ds(start, size), :] = value[:, out:]
        part = pl.ds(at(act_place + low), size)
        taps[part, pl.ds(out, 2 * out)] = value.astype(BF16)
        before = jnp.where(left, 0.0, odd[pl.ds(start - 1, size), :])
        after = jnp.where(right, 0.0, even[pl.ds(start + 1, size), :])
        taps[part, pl.ds(0, out)] = before.astype(BF16)
        taps[part, pl.ds(3 * out, out)] = after.astype(BF16)
    if not second:
        glob_edge[...] = glob_taps[pl.ds(at(1 + (half - 2) * (1 - side)), 2 * pairs), :]
        taps_edge[...] = taps[pl.ds(at(2 + (half - 4) * (1 - side)), 2 * pairs), :]
    writes = []
    for low, count in row_parts(rows, pairs):
        size = count * pairs
        value = pair_taps(taps, w_second_ref, low * pairs, size, pairs)
        value = silu(value + lifted_ref[pl.ds(at(first + low), size), :])
        start = 2 * low * pairs
        cells[pl.ds(start, size, stride=2), :] = value[:, :out]
        cells[pl.ds(start + 1, size, stride=2), :] = value[:, out:]
        for here, count in ((low, count // 2), (low + count // 2, count - count // 2)):
            part = pl.ds(here, count)
            value = cells[pl.ds(here * width, count * width), :].reshape(count, width, channels)
            resident = x_ref[pl.ds(first + here, count), :, :].astype(F32)
            out_ref[part, :, :] = (resident + value).astype(BF16)
            writes += start_copies(
                [(out_ref.at[part, :, :], out_hbm.at[pl.ds(first + here, count), :, :])],
                sems.at[pl.ds(len(writes), 1)],
            )
    for write in writes:
        write.wait()


def rest_part(second, side_of, place, flags, acc, lifted, x, w_second, w_glob, pieces, carried):
    _, width, channels = x.shape
    pairs = width // 2
    lanes = pieces[0].shape[1] // pairs
    half = pieces[0].shape[0] * len(pieces)
    rows = half + 2 if second else half
    space = pltpu.with_memory_space_constraint
    results = (pltpu.HBM(x.shape, BF16),)
    if not second:
        results += (
            pltpu.VMEM((2 * pairs, 2 * lanes), BF16),
            pltpu.VMEM((2 * pairs, 4 * channels), BF16),
        )
    return pl.pallas_call(
        lambda *refs: rest_kernel(second, side_of, place, *refs),
        out_shape=results,
        in_specs=in_vmem(6 + len(pieces))
        + (in_vmem(2) + in_hbm(1) if second else []),
        out_specs=tuple(in_hbm(1) + in_vmem(len(results) - 1)),
        input_output_aliases={8 + len(pieces): 0} if second else {},
        scratch_shapes=[
            pltpu.VMEM((rows, width, channels), BF16),
            pltpu.VMEM((half * pairs + 2 * EDGE, lanes), F32),
            pltpu.VMEM(((rows + 2) * pairs, 2 * lanes), BF16),
            pltpu.VMEM(((half + 1) * pairs + 2 * EDGE, channels), F32),
            pltpu.VMEM(((half + 1) * pairs + 2 * EDGE, channels), F32),
            pltpu.VMEM(((rows + 2) * pairs, 4 * channels), BF16),
            pltpu.VMEM((rows * width, channels), F32),
            pltpu.SemaphoreType.DMA((2 * len(row_parts(rows, pairs)),)),
        ],
        compiler_params=pltpu.CompilerParams(vmem_limit_bytes=VMEM_BYTES),
        cost_estimate=pl.CostEstimate(
            flops=4 * rows * width * 12 * channels * channels,
            bytes_accessed=4 * 1024 * 1024,
            transcendentals=0,
        ),
        name="rest_second" if second else "rest_first",
    )(
        *(space(a, pltpu.VMEM) for a in (flags, acc, lifted, x, w_second, w_glob)),
        *pieces,
        *carried,
    )


def rotated(block, axis, distance):
    count = lax.axis_size(axis)
    return lax.ppermute(block, axis, [(i, (i + distance) % count) for i in range(count)])


def swapped(block, bit):
    count = lax.axis_size("patch")
    return lax.ppermute(block, "patch", [(i, i ^ bit) for i in range(count)])


def side_first(away):
    return (away ^ (away >> 1)) & 1


def place_first(away, k):
    return ((away >> 1) ^ k) & 1


def per_device(
    features, context, owner, hours, w_first, w_second, w_lead_in, w_lead_mix, w_lead_out
):
    resident, block = features[0, 0], context[0, 0]
    acc, proj, flags, kept, w_second, w_glob, resident = resident_part(
        owner, resident, w_first, w_second, w_lead_in, block
    )

    def lifted_with(proj):
        before, after = rotated(proj, "lead", 1), rotated(proj, "lead", -1)
        return mix_part(hours, before, proj, after, w_lead_mix, w_lead_out)

    def rest(second, side_of, place, lifted, pieces, carried):
        return rest_part(second, side_of, place, flags, acc, lifted, resident, w_second, w_glob, pieces, carried)

    if lax.axis_size("patch") != 4:
        mine = lax.axis_index("patch") == owner[lax.axis_index("lead")]
        whole = lax.psum(jnp.where(mine, block, jnp.zeros_like(block)), "patch")
        result, _, _ = rest(
            False, lambda away: 0, lambda away, k: k, lifted_with(proj), [whole], []
        )
        return result[None, None]

    near, beside = flags[0] == 0, flags[1] == 0
    half = block.shape[0] // 2
    share = half // 2
    passing = swapped(block[half + share :], 1)
    staying = swapped(block[half : half + share], 1)
    passing, proj = lax.optimization_barrier((passing, proj))
    passing = jnp.where(near, kept[share:], passing)
    staying = jnp.where(near, kept[:share], staying)
    own = jnp.where(beside, staying, swapped(passing, 3))
    across = swapped(own, 3)
    lifted = lifted_with(proj)
    across, lifted = lax.optimization_barrier((across, lifted))
    upper = [own, across]
    lower = [swapped(own, 1), swapped(across, 1)]
    result, *edges = rest(False, side_first, place_first, lifted, upper, [])
    (result,) = rest(True, side_first, place_first, lifted, lower, [*edges, result])
    return result[None, None]


def solution(mesh):
    placed = (
        P(("grp", "lead"), "patch", None, None, None),
        P("patch", ("grp", "lead"), None, None),
        P("grp"),
        P("grp"),
        P(),
        P(),
        P(),
        P(),
        P(),
    )
    return jax.shard_map(
        per_device,
        mesh=mesh,
        in_specs=placed,
        out_specs=P(("grp", "lead"), "patch", None, None, None),
        check_vma=False,
    )
```

```python
import jax
import jax.numpy as jnp
from jax import lax
from jax.experimental import pallas as pl
from jax.experimental.pallas import tpu as pltpu
from jax.sharding import PartitionSpec as P

BF16 = jnp.bfloat16
F32 = jnp.float32
EDGE = 8
CHUNK = 256
WIDE = 1024
VMEM_BYTES = 20 * 1024 * 1024


def silu(v):
    return 0.5 * v * (1.0 + jnp.tanh(0.5 * v))


def dot(a, b):
    return jnp.dot(a, b, preferred_element_type=F32)


def dot_transposed(a, b):
    return lax.dot_general(a, b, (((1,), (1,)), ((), ())), preferred_element_type=F32)


def in_vmem(count):
    return [pl.BlockSpec(memory_space=pltpu.VMEM)] * count


def at_hbm(*arrays):
    return [pltpu.with_memory_space_constraint(a, pltpu.HBM) for a in arrays]


def in_hbm(count):
    return [pl.BlockSpec(memory_space=pltpu.HBM)] * count


def start_copies(pairs, sems):
    copies = [
        pltpu.make_async_copy(source, target, sems.at[k])
        for k, (source, target) in enumerate(pairs)
    ]
    for copy in copies:
        copy.start()
    return copies


def put_pair_weights(target, weights, first, depth, offsets):
    out = weights.shape[2]
    span = depth * len(offsets)
    for a in range(3):
        for place, d in enumerate(offsets):
            rows = pl.ds(a * span + place * depth, depth)
            for q in range(2):
                b = d - q + 1
                lanes = pl.ds(q * out, out)
                if 0 <= b <= 2:
                    target[rows, lanes] = weights[3 * a + b, pl.ds(first, depth), :]
                else:
                    target[rows, lanes] = jnp.zeros((depth, out), target.dtype)


def clear_edges(ref, pairs):
    zero = jnp.zeros((pairs, ref.shape[1]), ref.dtype)
    ref[pl.ds(0, pairs), :] = zero
    ref[pl.ds(ref.shape[0] - pairs, pairs), :] = zero


def pair_taps(taps, weights, start, size, pairs):
    depth = taps.shape[1]
    total = dot(taps[pl.ds(start, size), :], weights[pl.ds(0, depth), :])
    for a in range(1, 3):
        total += dot(
            taps[pl.ds(start + a * pairs, size), :], weights[pl.ds(a * depth, depth), :]
        )
    return total


def column_masks(size, lanes, pairs):
    m = lax.rem(lax.broadcasted_iota(jnp.int32, (size, lanes), 0), pairs)
    return m == 0, m == pairs - 1


def looped(count, body):
    lax.fori_loop(0, count, lambda k, carry: (body(k), carry)[1], 0)


def patches_away(owner_ref):
    return lax.axis_index("patch") ^ owner_ref[lax.axis_index("lead")]


def resident_kernel(
    owner_hbm, x_hbm, first_hbm, second_hbm, w_in_hbm, block_hbm,
    acc_ref, proj_ref, flags_ref, block_ref, w_second_ref, w_glob_ref, x_ref,
    first_ref, second_ref, in_ref, owner_ref, cells, taps, w_first, w_in, sems,
):
    height, width, channels = x_ref.shape
    pairs = width // 2
    rows = height * pairs
    temporal = in_ref.shape[0]
    glob = first_ref.shape[1] - channels
    parts = 4
    step = height // parts
    slices = [pl.ds(k * step, step) for k in range(parts)]
    copies = start_copies(
        [(x_hbm.at[part, :, :], x_ref.at[part, :, :]) for part in slices]
        + [
            (w_in_hbm, in_ref),
            (first_hbm, first_ref),
            (second_hbm, second_ref),
            (block_hbm.at[pl.ds(0, block_ref.shape[0]), :], block_ref),
            (owner_hbm, owner_ref),
        ],
        sems,
    )
    clear_edges(taps, pairs)
    w_in[...] = jnp.zeros_like(w_in)
    left, right = column_masks(CHUNK, channels, pairs)
    for k in range(parts):
        copies[k].wait()
        for start in range(k * step * pairs, (k + 1) * step * pairs, CHUNK):
            part = x_ref[pl.ds(start // pairs, CHUNK // pairs), :, :].astype(F32)
            cells[pl.ds(EDGE + 2 * start, 2 * CHUNK), :] = part.reshape(2 * CHUNK, channels)
            for place, d in enumerate((-1, 0, 1, 2)):
                value = cells[pl.ds(EDGE + 2 * start + d, CHUNK, stride=2), :]
                if d == -1:
                    value = jnp.where(left, 0.0, value)
                if d == 2:
                    value = jnp.where(right, 0.0, value)
                taps[pl.ds(pairs + start, CHUNK), pl.ds(place * channels, channels)] = value.astype(
                    BF16
                )
    half = rows // 2
    copies[parts].wait()
    for s in range(4):
        w_in[pl.ds(s * temporal, temporal), pl.ds(s * channels, channels)] = in_ref[...]
    for start in range(0, half, CHUNK):
        value = dot_transposed(
            taps[pl.ds(pairs + start, CHUNK), pl.ds(channels, 2 * channels)],
            w_in[:, pl.ds(0, 2 * channels)],
        ) + dot_transposed(
            taps[pl.ds(pairs + half + start, CHUNK), pl.ds(channels, 2 * channels)],
            w_in[:, pl.ds(2 * channels, 2 * channels)],
        )
        proj_ref[pl.ds(start, CHUNK), :] = value.astype(BF16)
    copies[parts + 1].wait()
    put_pair_weights(w_first, first_ref, 0, channels, (-1, 0, 1, 2))
    put_pair_weights(w_glob_ref, first_ref, channels, glob, (0, 1, 2, -1))
    copies[parts + 2].wait()
    put_pair_weights(w_second_ref, second_ref, 0, channels, (-1, 0, 1, 2))
    for start in range(0, rows, WIDE):
        acc_ref[pl.ds(start, WIDE), :] = pair_taps(taps, w_first, start, WIDE, pairs)
    copies[parts + 3].wait()
    copies[parts + 4].wait()
    away = patches_away(owner_ref)
    flags_ref[0] = jnp.full(flags_ref.shape[1:], away & 1, jnp.int32)
    flags_ref[1] = jnp.full(flags_ref.shape[1:], away & 2, jnp.int32)


def resident_part(owner, x, w_first, w_second, w_in, block):
    height, width, channels = x.shape
    out = w_first.shape[2]
    temporal = w_in.shape[1]
    w_in = w_in.T
    glob = w_first.shape[1] - channels
    pairs = width // 2
    rows = height * pairs
    results = (
        ((rows, 2 * out), F32),
        ((rows // 2, 4 * temporal), BF16),
        ((2, 1, width * glob), jnp.int32),
        ((height // 2, width * glob), BF16),
        ((12 * out, 2 * out), BF16),
        ((12 * glob, 2 * out), BF16),
        (x.shape, BF16),
    )
    return pl.pallas_call(
        resident_kernel,
        out_shape=tuple(
            space(*kind) for space, kind in zip((pltpu.VMEM,) * 7, results)
        ),
        in_specs=in_hbm(6),
        out_specs=tuple(in_vmem(7)),
        scratch_shapes=[
            pltpu.VMEM(w_first.shape, BF16),
            pltpu.VMEM(w_second.shape, BF16),
            pltpu.VMEM(w_in.shape, BF16),
            pltpu.SMEM(owner.shape, jnp.int32),
            pltpu.VMEM((2 * rows + 2 * EDGE, channels), F32),
            pltpu.VMEM((rows + 2 * pairs, 4 * channels), BF16),
            pltpu.VMEM((12 * channels, 2 * out), BF16),
            pltpu.VMEM((4 * temporal, 4 * channels), BF16),
            pltpu.SemaphoreType.DMA((9,)),
        ],
        compiler_params=pltpu.CompilerParams(vmem_limit_bytes=VMEM_BYTES),
        cost_estimate=pl.CostEstimate(flops=1024, bytes_accessed=1024, transcendentals=0),
        name="resident_part",
    )(*at_hbm(owner, x, w_first, w_second, w_in, block))


def mix_kernel(
    hours_hbm, prev_ref, self_ref, next_ref, mix_ref, out_ref, lifted_ref,
    w_mix, w_lift, mixed_ref, hours_ref, sem,
):
    hours_copy = pltpu.make_async_copy(hours_hbm, hours_ref, sem)
    hours_copy.start()
    temporal = mix_ref.shape[1]
    w_mix[...] = jnp.zeros_like(w_mix)
    for k in range(3):
        for s in range(4):
            w_mix[k, pl.ds(s * temporal, temporal), pl.ds(s * temporal, temporal)] = mix_ref[k]
    rows, out = mixed_ref.shape[0], out_ref.shape[1]
    w_lift[...] = jnp.zeros_like(w_lift)
    for s in range(2):
        for q in range(2):
            w_lift[
                s, pl.ds((2 * s + q) * temporal, temporal), pl.ds(q * out, out)
            ] = out_ref[...]
    hours_copy.wait()
    leads = hours_ref.shape[0]
    lead = lax.axis_index("lead")
    now = hours_ref[lead]
    before = hours_ref[jnp.maximum(lead - 1, 0)]
    after = hours_ref[jnp.minimum(lead + 1, leads - 1)]

    def gain(gap, used):
        gap = jnp.full((1, 4 * temporal), gap, jnp.int32).astype(F32)
        return jnp.where(used, jnp.exp(-0.5 * (gap - 1.0)), 0.0)

    gain_prev = gain(now - before, lead > 0)
    gain_next = gain(after - now, lead < leads - 1)
    for start in range(0, rows, CHUNK):
        part = pl.ds(start, CHUNK)
        value = gain_prev * dot(prev_ref[part, :], w_mix[0])
        value = value + dot(self_ref[part, :], w_mix[1])
        value = value + gain_next * dot(next_ref[part, :], w_mix[2])
        mixed_ref[part, :] = value.astype(BF16)
    for s in range(2):
        lifted_ref[pl.ds(s * rows, rows), :] = dot(mixed_ref[...], w_lift[s])


def mix_part(hours, before, own, after, w_mix, w_out):
    lanes, out = own.shape[1], w_out.shape[1]
    return pl.pallas_call(
        mix_kernel,
        out_shape=pltpu.VMEM((2 * own.shape[0], 2 * out), F32),
        in_specs=in_hbm(1) + in_vmem(5),
        out_specs=in_vmem(1)[0],
        scratch_shapes=[
            pltpu.VMEM((3, lanes, lanes), BF16),
            pltpu.VMEM((2, lanes, 2 * out), BF16),
            pltpu.VMEM(own.shape, BF16),
            pltpu.SMEM(hours.shape, jnp.int32),
            pltpu.SemaphoreType.DMA(()),
        ],
        compiler_params=pltpu.CompilerParams(vmem_limit_bytes=VMEM_BYTES),
        cost_estimate=pl.CostEstimate(
            flops=6 * own.shape[0] * lanes * lanes, bytes_accessed=1024 * 1024, transcendentals=0
        ),
        name="mix_part",
    )(*at_hbm(hours), before, own, after, w_mix, w_out)


def row_parts(rows, pairs):
    count = max(1, rows * pairs // CHUNK)
    bounds = [rows * k // count for k in range(count + 1)]
    return [(low, high - low) for low, high in zip(bounds, bounds[1:])]


def rest_kernel(second, side_of, place, flags_ref, acc_ref, lifted_ref, *refs):
    x_ref, w_second_ref, w_glob_ref, *refs = refs
    middle, refs = refs[:-8], refs[-8:]
    out_ref, glob_cells, glob_taps, odd, even, taps, cells, sems = refs
    if second:
        *pieces, glob_edge, taps_edge, _, out_hbm = middle
    else:
        *pieces, out_hbm, glob_edge, taps_edge = middle
    rows, width, channels = out_ref.shape
    pairs = width // 2
    out = channels
    lanes = glob_cells.shape[1]
    share = pieces[0].shape[0]
    half = share * len(pieces)
    away = jnp.max(flags_ref[0, :, :128]) + jnp.max(flags_ref[1, :, :128])
    side = side_of(away)
    first = (1 - side) * (half - 2) if second else side * half
    act_first = (1 - side) * (half - 1) if second else side * half
    act_rows = half + 1 if second else half
    act_place = 2 - side if second else 1
    new_place = 3 - 2 * side if second else 1

    def at(row):
        return pl.multiple_of(row * pairs, pairs)

    clear_edges(glob_taps, pairs)
    clear_edges(taps, pairs)
    for k, piece in enumerate(pieces):
        base = EDGE + at(place(away, k) * share)
        for m in range(pairs):
            value = piece[:, pl.ds(m * lanes, lanes)].astype(F32)
            glob_cells[pl.ds(base + m, share, stride=pairs), :] = value
    left, right = column_masks(CHUNK, lanes, pairs)
    lower = lax.broadcasted_iota(jnp.int32, (CHUNK, lanes), 1) < lanes // 2
    for start in range(0, half * pairs, CHUNK):
        here = glob_cells[pl.ds(EDGE + start, CHUNK), :]
        before = jnp.where(left, 0.0, glob_cells[pl.ds(EDGE - 1 + start, CHUNK), :])
        after = jnp.where(right, 0.0, glob_cells[pl.ds(EDGE + 1 + start, CHUNK), :])
        part = pl.ds(at(new_place + start // pairs), CHUNK)
        glob_taps[part, pl.ds(0, lanes)] = here.astype(BF16)
        glob_taps[part, pl.ds(lanes, lanes)] = jnp.where(lower, after, before).astype(BF16)
    if second:
        glob_taps[pl.ds(at(1 + half * side), 2 * pairs), :] = glob_edge[...]
        taps[pl.ds(at((half + 2) * side), 2 * pairs), :] = taps_edge[...]
    for low, count in row_parts(act_rows, pairs):
        size = count * pairs
        start = EDGE + low * pairs
        left, right = column_masks(size, out, pairs)
        value = acc_ref[pl.ds(at(act_first + low), size), :] + pair_taps(
            glob_taps, w_glob_ref, at(act_place + low - 1), size, pairs
        )
        value = silu(value)
        even[pl.ds(start, size), :] = value[:, :out]
        odd[pl.ds(start, size), :] = value[:, out:]
        part = pl.ds(at(act_place + low), size)
        taps[part, pl.ds(out, 2 * out)] = value.astype(BF16)
        before = jnp.where(left, 0.0, odd[pl.ds(start - 1, size), :])
        after = jnp.where(right, 0.0, even[pl.ds(start + 1, size), :])
        taps[part, pl.ds(0, out)] = before.astype(BF16)
        taps[part, pl.ds(3 * out, out)] = after.astype(BF16)
    if not second:
        glob_edge[...] = glob_taps[pl.ds(at(1 + (half - 2) * (1 - side)), 2 * pairs), :]
        taps_edge[...] = taps[pl.ds(at(2 + (half - 4) * (1 - side)), 2 * pairs), :]
    writes = []
    for low, count in row_parts(rows, pairs):
        size = count * pairs
        value = pair_taps(taps, w_second_ref, low * pairs, size, pairs)
        value = silu(value + lifted_ref[pl.ds(at(first + low), size), :])
        start = 2 * low * pairs
        cells[pl.ds(start, size, stride=2), :] = value[:, :out]
        cells[pl.ds(start + 1, size, stride=2), :] = value[:, out:]
        for here, count in ((low, count // 2), (low + count // 2, count - count // 2)):
            part = pl.ds(here, count)
            value = cells[pl.ds(here * width, count * width), :].reshape(count, width, channels)
            resident = x_ref[pl.ds(first + here, count), :, :].astype(F32)
            out_ref[part, :, :] = (resident + value).astype(BF16)
            writes += start_copies(
                [(out_ref.at[part, :, :], out_hbm.at[pl.ds(first + here, count), :, :])],
                sems.at[pl.ds(len(writes), 1)],
            )
    for write in writes:
        write.wait()


def rest_part(second, side_of, place, flags, acc, lifted, x, w_second, w_glob, pieces, carried):
    _, width, channels = x.shape
    pairs = width // 2
    lanes = pieces[0].shape[1] // pairs
    half = pieces[0].shape[0] * len(pieces)
    rows = half + 2 if second else half
    space = pltpu.with_memory_space_constraint
    results = (pltpu.HBM(x.shape, BF16),)
    if not second:
        results += (
            pltpu.VMEM((2 * pairs, 2 * lanes), BF16),
            pltpu.VMEM((2 * pairs, 4 * channels), BF16),
        )
    return pl.pallas_call(
        lambda *refs: rest_kernel(second, side_of, place, *refs),
        out_shape=results,
        in_specs=in_vmem(6 + len(pieces))
        + (in_vmem(2) + in_hbm(1) if second else []),
        out_specs=tuple(in_hbm(1) + in_vmem(len(results) - 1)),
        input_output_aliases={8 + len(pieces): 0} if second else {},
        scratch_shapes=[
            pltpu.VMEM((rows, width, channels), BF16),
            pltpu.VMEM(((half + 1) * pairs + 2 * EDGE, lanes), F32),
            pltpu.VMEM(((rows + 2) * pairs, 2 * lanes), BF16),
            pltpu.VMEM(((half + 1) * pairs + 2 * EDGE, channels), F32),
            pltpu.VMEM(((half + 1) * pairs + 2 * EDGE, channels), F32),
            pltpu.VMEM(((rows + 2) * pairs, 4 * channels), BF16),
            pltpu.VMEM((rows * width + EDGE, channels), F32),
            pltpu.SemaphoreType.DMA((2 * len(row_parts(rows, pairs)),)),
        ],
        compiler_params=pltpu.CompilerParams(vmem_limit_bytes=VMEM_BYTES),
        cost_estimate=pl.CostEstimate(
            flops=4 * rows * width * 12 * channels * channels,
            bytes_accessed=4 * 1024 * 1024,
            transcendentals=0,
        ),
        name="rest_second" if second else "rest_first",
    )(
        *(space(a, pltpu.VMEM) for a in (flags, acc, lifted, x, w_second, w_glob)),
        *pieces,
        *carried,
    )


def rotated(block, axis, distance):
    count = lax.axis_size(axis)
    return lax.ppermute(block, axis, [(i, (i + distance) % count) for i in range(count)])


def swapped(block, bit):
    count = lax.axis_size("patch")
    return lax.ppermute(block, "patch", [(i, i ^ bit) for i in range(count)])


def side_first(away):
    return (away ^ (away >> 1)) & 1


def place_first(away, k):
    return ((away >> 1) ^ k) & 1


def per_device(
    features, context, owner, hours, w_first, w_second, w_lead_in, w_lead_mix, w_lead_out
):
    resident, block = features[0, 0], context[0, 0]
    acc, proj, flags, kept, w_second, w_glob, resident = resident_part(
        owner, resident, w_first, w_second, w_lead_in, block
    )

    def lifted_with(proj):
        before, after = rotated(proj, "lead", 1), rotated(proj, "lead", -1)
        return mix_part(hours, before, proj, after, w_lead_mix, w_lead_out)

    def rest(second, side_of, place, lifted, pieces, carried):
        return rest_part(second, side_of, place, flags, acc, lifted, resident, w_second, w_glob, pieces, carried)

    if lax.axis_size("patch") != 4:
        mine = lax.axis_index("patch") == owner[lax.axis_index("lead")]
        whole = lax.psum(jnp.where(mine, block, jnp.zeros_like(block)), "patch")
        result, _, _ = rest(
            False, lambda away: 0, lambda away, k: k, lifted_with(proj), [whole], []
        )
        return result[None, None]

    near, beside = flags[0] == 0, flags[1] == 0
    half = block.shape[0] // 2
    share = half // 2
    passing = swapped(block[half + share :], 1)
    staying = swapped(block[half : half + share], 1)
    passing, proj = lax.optimization_barrier((passing, proj))
    passing = jnp.where(near, kept[share:], passing)
    staying = jnp.where(near, kept[:share], staying)
    own = jnp.where(beside, staying, swapped(passing, 3))
    across = swapped(own, 3)
    lifted = lifted_with(proj)
    across, lifted = lax.optimization_barrier((across, lifted))
    upper = [own, across]
    lower = [swapped(own, 1), swapped(across, 1)]
    result, *edges = rest(False, side_first, place_first, lifted, upper, [])
    (result,) = rest(True, side_first, place_first, lifted, lower, [*edges, result])
    return result[None, None]


def solution(mesh):
    placed = (
        P(("grp", "lead"), "patch", None, None, None),
        P("patch", ("grp", "lead"), None, None),
        P("grp"),
        P("grp"),
        P(),
        P(),
        P(),
        P(),
        P(),
    )
    return jax.shard_map(
        per_device,
        mesh=mesh,
        in_specs=placed,
        out_specs=P(("grp", "lead"), "patch", None, None, None),
        check_vma=False,
    )
```

```python
import jax
import jax.numpy as jnp
from jax import lax
from jax.experimental import pallas as pl
from jax.experimental.pallas import tpu as pltpu
from jax.sharding import PartitionSpec as P

BF16 = jnp.bfloat16
F32 = jnp.float32
EDGE = 8
CHUNK = 256
WIDE = 1024
VMEM_BYTES = 20 * 1024 * 1024


def silu(v):
    return 0.5 * v * (1.0 + jnp.tanh(0.5 * v))


def dot(a, b):
    return jnp.dot(a, b, preferred_element_type=F32)


def dot_transposed(a, b):
    return lax.dot_general(a, b, (((1,), (1,)), ((), ())), preferred_element_type=F32)


def in_vmem(count):
    return [pl.BlockSpec(memory_space=pltpu.VMEM)] * count


def at_hbm(*arrays):
    return [pltpu.with_memory_space_constraint(a, pltpu.HBM) for a in arrays]


def in_hbm(count):
    return [pl.BlockSpec(memory_space=pltpu.HBM)] * count


def start_copies(pairs, sems):
    copies = [
        pltpu.make_async_copy(source, target, sems.at[k])
        for k, (source, target) in enumerate(pairs)
    ]
    for copy in copies:
        copy.start()
    return copies


def put_pair_weights(target, weights, first, depth, offsets):
    out = weights.shape[2]
    span = depth * len(offsets)
    for a in range(3):
        for place, d in enumerate(offsets):
            rows = pl.ds(a * span + place * depth, depth)
            for q in range(2):
                b = d - q + 1
                lanes = pl.ds(q * out, out)
                if 0 <= b <= 2:
                    target[rows, lanes] = weights[3 * a + b, pl.ds(first, depth), :]
                else:
                    target[rows, lanes] = jnp.zeros((depth, out), target.dtype)


def clear_edges(ref, pairs):
    zero = jnp.zeros((pairs, ref.shape[1]), ref.dtype)
    ref[pl.ds(0, pairs), :] = zero
    ref[pl.ds(ref.shape[0] - pairs, pairs), :] = zero


def pair_taps(taps, weights, start, size, pairs):
    depth = taps.shape[1]
    total = dot(taps[pl.ds(start, size), :], weights[pl.ds(0, depth), :])
    for a in range(1, 3):
        total += dot(
            taps[pl.ds(start + a * pairs, size), :], weights[pl.ds(a * depth, depth), :]
        )
    return total


def column_masks(size, lanes, pairs):
    m = lax.rem(lax.broadcasted_iota(jnp.int32, (size, lanes), 0), pairs)
    return m == 0, m == pairs - 1


def looped(count, body):
    lax.fori_loop(0, count, lambda k, carry: (body(k), carry)[1], 0)


def patches_away(owner_ref):
    return lax.axis_index("patch") ^ owner_ref[lax.axis_index("lead")]


def resident_kernel(
    owner_hbm, x_hbm, first_hbm, second_hbm, w_in_hbm, block_hbm,
    acc_ref, proj_ref, flags_ref, block_ref, w_second_ref, w_glob_ref, x_ref,
    first_ref, second_ref, in_ref, owner_ref, cells, taps, w_first, w_in, sems,
):
    height, width, channels = x_ref.shape
    pairs = width // 2
    rows = height * pairs
    temporal = in_ref.shape[0]
    glob = first_ref.shape[1] - channels
    parts = 4
    step = height // parts
    slices = [pl.ds(k * step, step) for k in range(parts)]
    copies = start_copies(
        [(x_hbm.at[part, :, :], x_ref.at[part, :, :]) for part in slices]
        + [
            (w_in_hbm, in_ref),
            (first_hbm, first_ref),
            (second_hbm, second_ref),
            (block_hbm.at[pl.ds(0, block_ref.shape[0]), :], block_ref),
            (owner_hbm, owner_ref),
        ],
        sems,
    )
    clear_edges(taps, pairs)
    w_in[...] = jnp.zeros_like(w_in)
    left, right = column_masks(CHUNK, channels, pairs)
    for k in range(parts):
        copies[k].wait()
        for start in range(k * step * pairs, (k + 1) * step * pairs, CHUNK):
            part = x_ref[pl.ds(start // pairs, CHUNK // pairs), :, :].astype(F32)
            cells[pl.ds(EDGE + 2 * start, 2 * CHUNK), :] = part.reshape(2 * CHUNK, channels)
            for place, d in enumerate((-1, 0, 1, 2)):
                value = cells[pl.ds(EDGE + 2 * start + d, CHUNK, stride=2), :]
                if d == -1:
                    value = jnp.where(left, 0.0, value)
                if d == 2:
                    value = jnp.where(right, 0.0, value)
                taps[pl.ds(pairs + start, CHUNK), pl.ds(place * channels, channels)] = value.astype(
                    BF16
                )
    half = rows // 2
    copies[parts].wait()
    for s in range(4):
        w_in[pl.ds(s * temporal, temporal), pl.ds(s * channels, channels)] = in_ref[...]
    for start in range(0, half, CHUNK):
        value = dot_transposed(
            taps[pl.ds(pairs + start, CHUNK), pl.ds(channels, 2 * channels)],
            w_in[:, pl.ds(0, 2 * channels)],
        ) + dot_transposed(
            taps[pl.ds(pairs + half + start, CHUNK), pl.ds(channels, 2 * channels)],
            w_in[:, pl.ds(2 * channels, 2 * channels)],
        )
        proj_ref[pl.ds(start, CHUNK), :] = value.astype(BF16)
    copies[parts + 1].wait()
    put_pair_weights(w_first, first_ref, 0, channels, (-1, 0, 1, 2))
    put_pair_weights(w_glob_ref, first_ref, channels, glob, (0, 1, 2, -1))
    copies[parts + 2].wait()
    put_pair_weights(w_second_ref, second_ref, 0, channels, (-1, 0, 1, 2))
    for start in range(0, rows, WIDE):
        acc_ref[pl.ds(start, WIDE), :] = pair_taps(taps, w_first, start, WIDE, pairs)
    copies[parts + 3].wait()
    copies[parts + 4].wait()
    away = patches_away(owner_ref)
    flags_ref[0] = jnp.full(flags_ref.shape[1:], away & 1, jnp.int32)
    flags_ref[1] = jnp.full(flags_ref.shape[1:], away & 2, jnp.int32)


def resident_part(owner, x, w_first, w_second, w_in, block):
    height, width, channels = x.shape
    out = w_first.shape[2]
    temporal = w_in.shape[1]
    w_in = w_in.T
    glob = w_first.shape[1] - channels
    pairs = width // 2
    rows = height * pairs
    results = (
        ((rows, 2 * out), F32),
        ((rows // 2, 4 * temporal), BF16),
        ((2, 1, width * glob), jnp.int32),
        ((height // 2, width * glob), BF16),
        ((12 * out, 2 * out), BF16),
        ((12 * glob, 2 * out), BF16),
        (x.shape, BF16),
    )
    return pl.pallas_call(
        resident_kernel,
        out_shape=tuple(
            space(*kind) for space, kind in zip((pltpu.VMEM,) * 7, results)
        ),
        in_specs=in_hbm(6),
        out_specs=tuple(in_vmem(7)),
        scratch_shapes=[
            pltpu.VMEM(w_first.shape, BF16),
            pltpu.VMEM(w_second.shape, BF16),
            pltpu.VMEM(w_in.shape, BF16),
            pltpu.SMEM(owner.shape, jnp.int32),
            pltpu.VMEM((2 * rows + 2 * EDGE, channels), F32),
            pltpu.VMEM((rows + 2 * pairs, 4 * channels), BF16),
            pltpu.VMEM((12 * channels, 2 * out), BF16),
            pltpu.VMEM((4 * temporal, 4 * channels), BF16),
            pltpu.SemaphoreType.DMA((9,)),
        ],
        compiler_params=pltpu.CompilerParams(vmem_limit_bytes=VMEM_BYTES),
        cost_estimate=pl.CostEstimate(flops=1024, bytes_accessed=1024, transcendentals=0),
        name="resident_part",
    )(*at_hbm(owner, x, w_first, w_second, w_in, block))


def mix_kernel(
    hours_hbm, prev_ref, self_ref, next_ref, mix_ref, out_ref, lifted_ref,
    w_mix, w_lift, mixed_ref, hours_ref, sem,
):
    hours_copy = pltpu.make_async_copy(hours_hbm, hours_ref, sem)
    hours_copy.start()
    temporal = mix_ref.shape[1]
    w_mix[...] = jnp.zeros_like(w_mix)
    for k in range(3):
        for s in range(4):
            w_mix[k, pl.ds(s * temporal, temporal), pl.ds(s * temporal, temporal)] = mix_ref[k]
    rows, out = mixed_ref.shape[0], out_ref.shape[1]
    w_lift[...] = jnp.zeros_like(w_lift)
    for s in range(2):
        for q in range(2):
            w_lift[
                s, pl.ds((2 * s + q) * temporal, temporal), pl.ds(q * out, out)
            ] = out_ref[...]
    hours_copy.wait()
    leads = hours_ref.shape[0]
    lead = lax.axis_index("lead")
    now = hours_ref[lead]
    before = hours_ref[jnp.maximum(lead - 1, 0)]
    after = hours_ref[jnp.minimum(lead + 1, leads - 1)]

    def gain(gap, used):
        gap = jnp.full((1, 4 * temporal), gap, jnp.int32).astype(F32)
        return jnp.where(used, jnp.exp(-0.5 * (gap - 1.0)), 0.0)

    gain_prev = gain(now - before, lead > 0)
    gain_next = gain(after - now, lead < leads - 1)
    for start in range(0, rows, CHUNK):
        part = pl.ds(start, CHUNK)
        value = gain_prev * dot(prev_ref[part, :], w_mix[0])
        value = value + dot(self_ref[part, :], w_mix[1])
        value = value + gain_next * dot(next_ref[part, :], w_mix[2])
        mixed_ref[part, :] = value.astype(BF16)
    for s in range(2):
        lifted_ref[pl.ds(s * rows, rows), :] = dot(mixed_ref[...], w_lift[s])


def mix_part(hours, before, own, after, w_mix, w_out):
    lanes, out = own.shape[1], w_out.shape[1]
    return pl.pallas_call(
        mix_kernel,
        out_shape=pltpu.VMEM((2 * own.shape[0], 2 * out), F32),
        in_specs=in_hbm(1) + in_vmem(5),
        out_specs=in_vmem(1)[0],
        scratch_shapes=[
            pltpu.VMEM((3, lanes, lanes), BF16),
            pltpu.VMEM((2, lanes, 2 * out), BF16),
            pltpu.VMEM(own.shape, BF16),
            pltpu.SMEM(hours.shape, jnp.int32),
            pltpu.SemaphoreType.DMA(()),
        ],
        compiler_params=pltpu.CompilerParams(vmem_limit_bytes=VMEM_BYTES),
        cost_estimate=pl.CostEstimate(
            flops=6 * own.shape[0] * lanes * lanes, bytes_accessed=1024 * 1024, transcendentals=0
        ),
        name="mix_part",
    )(*at_hbm(hours), before, own, after, w_mix, w_out)


def row_parts(rows, pairs):
    count = max(1, rows * pairs // CHUNK)
    bounds = [rows * k // count for k in range(count + 1)]
    return [(low, high - low) for low, high in zip(bounds, bounds[1:])]


def rest_kernel(second, side_of, place, flags_ref, acc_ref, lifted_ref, *refs):
    x_ref, w_second_ref, w_glob_ref, *refs = refs
    middle, refs = refs[:-6], refs[-6:]
    out_ref, glob_cells, glob_taps, taps, cells, sems = refs
    if second:
        *pieces, glob_edge, taps_edge, _, out_hbm = middle
    else:
        *pieces, out_hbm, glob_edge, taps_edge = middle
    rows, width, channels = out_ref.shape
    pairs = width // 2
    out = channels
    lanes = glob_cells.shape[1]
    share = pieces[0].shape[0]
    half = share * len(pieces)
    away = jnp.max(flags_ref[0, :, :128]) + jnp.max(flags_ref[1, :, :128])
    side = side_of(away)
    first = (1 - side) * (half - 2) if second else side * half
    act_first = (1 - side) * (half - 1) if second else side * half
    act_rows = half + 1 if second else half
    act_place = 2 - side if second else 1
    new_place = 3 - 2 * side if second else 1

    def at(row):
        return pl.multiple_of(row * pairs, pairs)

    clear_edges(glob_taps, pairs)
    clear_edges(taps, pairs)
    for k, piece in enumerate(pieces):
        base = EDGE + at(place(away, k) * share)
        for m in range(pairs):
            value = piece[:, pl.ds(m * lanes, lanes)].astype(F32)
            glob_cells[pl.ds(base + m, share, stride=pairs), :] = value
    left, right = column_masks(CHUNK, lanes, pairs)
    lower = lax.broadcasted_iota(jnp.int32, (CHUNK, lanes), 1) < lanes // 2
    for start in range(0, half * pairs, CHUNK):
        here = glob_cells[pl.ds(EDGE + start, CHUNK), :]
        before = jnp.where(left, 0.0, glob_cells[pl.ds(EDGE - 1 + start, CHUNK), :])
        after = jnp.where(right, 0.0, glob_cells[pl.ds(EDGE + 1 + start, CHUNK), :])
        part = pl.ds(at(new_place + start // pairs), CHUNK)
        glob_taps[part, pl.ds(0, lanes)] = here.astype(BF16)
        glob_taps[part, pl.ds(lanes, lanes)] = jnp.where(lower, after, before).astype(BF16)
    if second:
        glob_taps[pl.ds(at(1 + half * side), 2 * pairs), :] = glob_edge[...]
        taps[pl.ds(at((half + 2) * side), 2 * pairs), :] = taps_edge[...]
    for low, count in row_parts(act_rows, pairs):
        size = count * pairs
        left, right = column_masks(size, out, pairs)
        value = acc_ref[pl.ds(at(act_first + low), size), :] + pair_taps(
            glob_taps, w_glob_ref, at(act_place + low - 1), size, pairs
        )
        value = silu(value)
        part = pl.ds(at(act_place + low), size)
        taps[part, pl.ds(out, 2 * out)] = value.astype(BF16)
        before = jnp.where(left, 0.0, pltpu.roll(value[:, out:], 1, 0))
        after = jnp.where(right, 0.0, pltpu.roll(value[:, :out], size - 1, 0))
        taps[part, pl.ds(0, out)] = before.astype(BF16)
        taps[part, pl.ds(3 * out, out)] = after.astype(BF16)
    if not second:
        glob_edge[...] = glob_taps[pl.ds(at(1 + (half - 2) * (1 - side)), 2 * pairs), :]
        taps_edge[...] = taps[pl.ds(at(2 + (half - 4) * (1 - side)), 2 * pairs), :]
    writes = []
    for low, count in row_parts(rows, pairs):
        size = count * pairs
        value = pair_taps(taps, w_second_ref, low * pairs, size, pairs)
        value = silu(value + lifted_ref[pl.ds(at(first + low), size), :])
        start = 2 * low * pairs
        cells[pl.ds(start, size, stride=2), :] = value[:, :out]
        cells[pl.ds(start + 1, size, stride=2), :] = value[:, out:]
        for here, count in ((low, count // 2), (low + count // 2, count - count // 2)):
            part = pl.ds(here, count)
            value = cells[pl.ds(here * width, count * width), :].reshape(count, width, channels)
            resident = x_ref[pl.ds(first + here, count), :, :].astype(F32)
            out_ref[part, :, :] = (resident + value).astype(BF16)
            writes += start_copies(
                [(out_ref.at[part, :, :], out_hbm.at[pl.ds(first + here, count), :, :])],
                sems.at[pl.ds(len(writes), 1)],
            )
    for write in writes:
        write.wait()


def rest_part(second, side_of, place, flags, acc, lifted, x, w_second, w_glob, pieces, carried):
    _, width, channels = x.shape
    pairs = width // 2
    lanes = pieces[0].shape[1] // pairs
    half = pieces[0].shape[0] * len(pieces)
    rows = half + 2 if second else half
    space = pltpu.with_memory_space_constraint
    results = (pltpu.HBM(x.shape, BF16),)
    if not second:
        results += (
            pltpu.VMEM((2 * pairs, 2 * lanes), BF16),
            pltpu.VMEM((2 * pairs, 4 * channels), BF16),
        )
    return pl.pallas_call(
        lambda *refs: rest_kernel(second, side_of, place, *refs),
        out_shape=results,
        in_specs=in_vmem(6 + len(pieces))
        + (in_vmem(2) + in_hbm(1) if second else []),
        out_specs=tuple(in_hbm(1) + in_vmem(len(results) - 1)),
        input_output_aliases={8 + len(pieces): 0} if second else {},
        scratch_shapes=[
            pltpu.VMEM((rows, width, channels), BF16),
            pltpu.VMEM(((half + 1) * pairs + 2 * EDGE, lanes), F32),
            pltpu.VMEM(((rows + 2) * pairs, 2 * lanes), BF16),
            pltpu.VMEM(((rows + 2) * pairs, 4 * channels), BF16),
            pltpu.VMEM((rows * width + EDGE, channels), F32),
            pltpu.SemaphoreType.DMA((2 * len(row_parts(rows, pairs)),)),
        ],
        compiler_params=pltpu.CompilerParams(vmem_limit_bytes=VMEM_BYTES),
        cost_estimate=pl.CostEstimate(
            flops=4 * rows * width * 12 * channels * channels,
            bytes_accessed=4 * 1024 * 1024,
            transcendentals=0,
        ),
        name="rest_second" if second else "rest_first",
    )(
        *(space(a, pltpu.VMEM) for a in (flags, acc, lifted, x, w_second, w_glob)),
        *pieces,
        *carried,
    )


def rotated(block, axis, distance):
    count = lax.axis_size(axis)
    return lax.ppermute(block, axis, [(i, (i + distance) % count) for i in range(count)])


def swapped(block, bit):
    count = lax.axis_size("patch")
    return lax.ppermute(block, "patch", [(i, i ^ bit) for i in range(count)])


def side_first(away):
    return (away ^ (away >> 1)) & 1


def place_first(away, k):
    return ((away >> 1) ^ k) & 1


def per_device(
    features, context, owner, hours, w_first, w_second, w_lead_in, w_lead_mix, w_lead_out
):
    resident, block = features[0, 0], context[0, 0]
    acc, proj, flags, kept, w_second, w_glob, resident = resident_part(
        owner, resident, w_first, w_second, w_lead_in, block
    )

    def lifted_with(proj):
        before, after = rotated(proj, "lead", 1), rotated(proj, "lead", -1)
        return mix_part(hours, before, proj, after, w_lead_mix, w_lead_out)

    def rest(second, side_of, place, lifted, pieces, carried):
        return rest_part(second, side_of, place, flags, acc, lifted, resident, w_second, w_glob, pieces, carried)

    if lax.axis_size("patch") != 4:
        mine = lax.axis_index("patch") == owner[lax.axis_index("lead")]
        whole = lax.psum(jnp.where(mine, block, jnp.zeros_like(block)), "patch")
        result, _, _ = rest(
            False, lambda away: 0, lambda away, k: k, lifted_with(proj), [whole], []
        )
        return result[None, None]

    near, beside = flags[0] == 0, flags[1] == 0
    half = block.shape[0] // 2
    share = half // 2
    passing = swapped(block[half + share :], 1)
    staying = swapped(block[half : half + share], 1)
    passing, proj = lax.optimization_barrier((passing, proj))
    passing = jnp.where(near, kept[share:], passing)
    staying = jnp.where(near, kept[:share], staying)
    own = jnp.where(beside, staying, swapped(passing, 3))
    across = swapped(own, 3)
    lifted = lifted_with(proj)
    across, lifted = lax.optimization_barrier((across, lifted))
    upper = [own, across]
    lower = [swapped(own, 1), swapped(across, 1)]
    result, *edges = rest(False, side_first, place_first, lifted, upper, [])
    (result,) = rest(True, side_first, place_first, lifted, lower, [*edges, result])
    return result[None, None]


def solution(mesh):
    placed = (
        P(("grp", "lead"), "patch", None, None, None),
        P("patch", ("grp", "lead"), None, None),
        P("grp"),
        P("grp"),
        P(),
        P(),
        P(),
        P(),
        P(),
    )
    return jax.shard_map(
        per_device,
        mesh=mesh,
        in_specs=placed,
        out_specs=P(("grp", "lead"), "patch", None, None, None),
        check_vma=False,
    )
```

```python
import jax
import jax.numpy as jnp
from jax import lax
from jax.experimental import pallas as pl
from jax.experimental.pallas import tpu as pltpu
from jax.sharding import PartitionSpec as P

BF16 = jnp.bfloat16
F32 = jnp.float32
EDGE = 8
CHUNK = 256
WIDE = 1024
VMEM_BYTES = 20 * 1024 * 1024


def silu(v):
    return 0.5 * v * (1.0 + jnp.tanh(0.5 * v))


def dot(a, b):
    return jnp.dot(a, b, preferred_element_type=F32)


def dot_transposed(a, b):
    return lax.dot_general(a, b, (((1,), (1,)), ((), ())), preferred_element_type=F32)


def in_vmem(count):
    return [pl.BlockSpec(memory_space=pltpu.VMEM)] * count


def at_hbm(*arrays):
    return [pltpu.with_memory_space_constraint(a, pltpu.HBM) for a in arrays]


def in_hbm(count):
    return [pl.BlockSpec(memory_space=pltpu.HBM)] * count


def start_copies(pairs, sems):
    copies = [
        pltpu.make_async_copy(source, target, sems.at[k])
        for k, (source, target) in enumerate(pairs)
    ]
    for copy in copies:
        copy.start()
    return copies


def put_pair_weights(target, weights, first, depth, offsets):
    out = weights.shape[2]
    span = depth * len(offsets)
    for a in range(3):
        for place, d in enumerate(offsets):
            rows = pl.ds(a * span + place * depth, depth)
            for q in range(2):
                b = d - q + 1
                lanes = pl.ds(q * out, out)
                if 0 <= b <= 2:
                    target[rows, lanes] = weights[3 * a + b, pl.ds(first, depth), :]
                else:
                    target[rows, lanes] = jnp.zeros((depth, out), target.dtype)


def clear_edges(ref, pairs):
    zero = jnp.zeros((pairs, ref.shape[1]), ref.dtype)
    ref[pl.ds(0, pairs), :] = zero
    ref[pl.ds(ref.shape[0] - pairs, pairs), :] = zero


def pair_taps(taps, weights, start, size, pairs):
    depth = taps.shape[1]
    total = dot(taps[pl.ds(start, size), :], weights[pl.ds(0, depth), :])
    for a in range(1, 3):
        total += dot(
            taps[pl.ds(start + a * pairs, size), :], weights[pl.ds(a * depth, depth), :]
        )
    return total


def column_masks(size, lanes, pairs):
    m = lax.rem(lax.broadcasted_iota(jnp.int32, (size, lanes), 0), pairs)
    return m == 0, m == pairs - 1


def looped(count, body):
    lax.fori_loop(0, count, lambda k, carry: (body(k), carry)[1], 0)


def patches_away(owner_ref):
    return lax.axis_index("patch") ^ owner_ref[lax.axis_index("lead")]


def resident_kernel(
    owner_hbm, x_hbm, first_hbm, second_hbm, w_in_hbm, block_hbm,
    acc_ref, proj_ref, flags_ref, block_ref, w_second_ref, w_glob_ref, x_ref,
    first_ref, second_ref, in_ref, owner_ref, cells, taps, w_first, w_in, sems,
):
    height, width, channels = x_ref.shape
    pairs = width // 2
    rows = height * pairs
    temporal = in_ref.shape[0]
    glob = first_ref.shape[1] - channels
    parts = 4
    step = height // parts
    slices = [pl.ds(k * step, step) for k in range(parts)]
    copies = start_copies(
        [(x_hbm.at[part, :, :], x_ref.at[part, :, :]) for part in slices]
        + [
            (w_in_hbm, in_ref),
            (first_hbm, first_ref),
            (second_hbm, second_ref),
            (block_hbm.at[pl.ds(0, block_ref.shape[0]), :], block_ref),
            (owner_hbm, owner_ref),
        ],
        sems,
    )
    clear_edges(taps, pairs)
    w_in[...] = jnp.zeros_like(w_in)
    left, right = column_masks(CHUNK, channels, pairs)
    for k in range(parts):
        copies[k].wait()
        for start in range(k * step * pairs, (k + 1) * step * pairs, CHUNK):
            part = x_ref[pl.ds(start // pairs, CHUNK // pairs), :, :].astype(F32)
            cells[pl.ds(EDGE + 2 * start, 2 * CHUNK), :] = part.reshape(2 * CHUNK, channels)
            for place, d in enumerate((-1, 0, 1, 2)):
                value = cells[pl.ds(EDGE + 2 * start + d, CHUNK, stride=2), :]
                if d == -1:
                    value = jnp.where(left, 0.0, value)
                if d == 2:
                    value = jnp.where(right, 0.0, value)
                taps[pl.ds(pairs + start, CHUNK), pl.ds(place * channels, channels)] = value.astype(
                    BF16
                )
    half = rows // 2
    copies[parts].wait()
    for s in range(4):
        w_in[pl.ds(s * temporal, temporal), pl.ds(s * channels, channels)] = in_ref[...]
    for start in range(0, half, CHUNK):
        value = dot_transposed(
            taps[pl.ds(pairs + start, CHUNK), pl.ds(channels, 2 * channels)],
            w_in[:, pl.ds(0, 2 * channels)],
        ) + dot_transposed(
            taps[pl.ds(pairs + half + start, CHUNK), pl.ds(channels, 2 * channels)],
            w_in[:, pl.ds(2 * channels, 2 * channels)],
        )
        proj_ref[pl.ds(start, CHUNK), :] = value.astype(BF16)
    copies[parts + 1].wait()
    put_pair_weights(w_first, first_ref, 0, channels, (-1, 0, 1, 2))
    put_pair_weights(w_glob_ref, first_ref, channels, glob, (0, 1, 2, -1))
    copies[parts + 2].wait()
    put_pair_weights(w_second_ref, second_ref, 0, channels, (-1, 0, 1, 2))
    for start in range(0, rows, WIDE):
        acc_ref[pl.ds(start, WIDE), :] = pair_taps(taps, w_first, start, WIDE, pairs)
    copies[parts + 3].wait()
    copies[parts + 4].wait()
    away = patches_away(owner_ref)
    flags_ref[0] = jnp.full(flags_ref.shape[1:], away & 1, jnp.int32)
    flags_ref[1] = jnp.full(flags_ref.shape[1:], away & 2, jnp.int32)


def resident_part(owner, x, w_first, w_second, w_in, block):
    height, width, channels = x.shape
    out = w_first.shape[2]
    temporal = w_in.shape[1]
    w_in = w_in.T
    glob = w_first.shape[1] - channels
    pairs = width // 2
    rows = height * pairs
    results = (
        ((rows, 2 * out), F32),
        ((rows // 2, 4 * temporal), BF16),
        ((2, 1, width * glob), jnp.int32),
        ((height // 2, width * glob), BF16),
        ((12 * out, 2 * out), BF16),
        ((12 * glob, 2 * out), BF16),
        (x.shape, BF16),
    )
    return pl.pallas_call(
        resident_kernel,
        out_shape=tuple(
            space(*kind) for space, kind in zip((pltpu.VMEM,) * 7, results)
        ),
        in_specs=in_hbm(6),
        out_specs=tuple(in_vmem(7)),
        scratch_shapes=[
            pltpu.VMEM(w_first.shape, BF16),
            pltpu.VMEM(w_second.shape, BF16),
            pltpu.VMEM(w_in.shape, BF16),
            pltpu.SMEM(owner.shape, jnp.int32),
            pltpu.VMEM((2 * rows + 2 * EDGE, channels), F32),
            pltpu.VMEM((rows + 2 * pairs, 4 * channels), BF16),
            pltpu.VMEM((12 * channels, 2 * out), BF16),
            pltpu.VMEM((4 * temporal, 4 * channels), BF16),
            pltpu.SemaphoreType.DMA((9,)),
        ],
        compiler_params=pltpu.CompilerParams(vmem_limit_bytes=VMEM_BYTES),
        cost_estimate=pl.CostEstimate(flops=1024, bytes_accessed=1024, transcendentals=0),
        name="resident_part",
    )(*at_hbm(owner, x, w_first, w_second, w_in, block))


def mix_kernel(
    hours_hbm, prev_ref, self_ref, next_ref, mix_ref, out_ref, lifted_ref,
    w_mix, w_lift, mixed_ref, hours_ref, sem,
):
    hours_copy = pltpu.make_async_copy(hours_hbm, hours_ref, sem)
    hours_copy.start()
    temporal = mix_ref.shape[1]
    w_mix[...] = jnp.zeros_like(w_mix)
    for k in range(3):
        for s in range(4):
            w_mix[k, pl.ds(s * temporal, temporal), pl.ds(s * temporal, temporal)] = mix_ref[k]
    rows, out = mixed_ref.shape[0], out_ref.shape[1]
    w_lift[...] = jnp.zeros_like(w_lift)
    for s in range(2):
        for q in range(2):
            w_lift[
                s, pl.ds((2 * s + q) * temporal, temporal), pl.ds(q * out, out)
            ] = out_ref[...]
    hours_copy.wait()
    leads = hours_ref.shape[0]
    lead = lax.axis_index("lead")
    now = hours_ref[lead]
    before = hours_ref[jnp.maximum(lead - 1, 0)]
    after = hours_ref[jnp.minimum(lead + 1, leads - 1)]

    def gain(gap, used):
        gap = jnp.full((1, 4 * temporal), gap, jnp.int32).astype(F32)
        return jnp.where(used, jnp.exp(-0.5 * (gap - 1.0)), 0.0)

    gain_prev = gain(now - before, lead > 0)
    gain_next = gain(after - now, lead < leads - 1)
    for start in range(0, rows, CHUNK):
        part = pl.ds(start, CHUNK)
        value = gain_prev * dot(prev_ref[part, :], w_mix[0])
        value = value + dot(self_ref[part, :], w_mix[1])
        value = value + gain_next * dot(next_ref[part, :], w_mix[2])
        mixed_ref[part, :] = value.astype(BF16)
    for s in range(2):
        lifted_ref[pl.ds(s * rows, rows), :] = dot(mixed_ref[...], w_lift[s])


def mix_part(hours, before, own, after, w_mix, w_out):
    lanes, out = own.shape[1], w_out.shape[1]
    return pl.pallas_call(
        mix_kernel,
        out_shape=pltpu.VMEM((2 * own.shape[0], 2 * out), F32),
        in_specs=in_hbm(1) + in_vmem(5),
        out_specs=in_vmem(1)[0],
        scratch_shapes=[
            pltpu.VMEM((3, lanes, lanes), BF16),
            pltpu.VMEM((2, lanes, 2 * out), BF16),
            pltpu.VMEM(own.shape, BF16),
            pltpu.SMEM(hours.shape, jnp.int32),
            pltpu.SemaphoreType.DMA(()),
        ],
        compiler_params=pltpu.CompilerParams(vmem_limit_bytes=VMEM_BYTES),
        cost_estimate=pl.CostEstimate(
            flops=6 * own.shape[0] * lanes * lanes, bytes_accessed=1024 * 1024, transcendentals=0
        ),
        name="mix_part",
    )(*at_hbm(hours), before, own, after, w_mix, w_out)


def row_parts(rows, pairs):
    count = max(1, rows * pairs // CHUNK)
    bounds = [rows * k // count for k in range(count + 1)]
    return [(low, high - low) for low, high in zip(bounds, bounds[1:])]


def rest_kernel(second, side_of, place, flags_ref, acc_ref, lifted_ref, *refs):
    x_ref, w_second_ref, w_glob_ref, *refs = refs
    middle, refs = refs[:-6], refs[-6:]
    out_ref, glob_cells, glob_taps, taps, cells, sems = refs
    if second:
        *pieces, glob_edge, taps_edge, _, out_hbm = middle
    else:
        *pieces, out_hbm, glob_edge, taps_edge = middle
    rows, width, channels = out_ref.shape
    pairs = width // 2
    out = channels
    lanes = glob_cells.shape[1]
    share = pieces[0].shape[0]
    half = share * len(pieces)
    away = jnp.max(flags_ref[0, :, :128]) + jnp.max(flags_ref[1, :, :128])
    side = side_of(away)
    first = (1 - side) * (half - 2) if second else side * half
    act_first = (1 - side) * (half - 1) if second else side * half
    act_rows = half + 1 if second else half
    act_place = 2 - side if second else 1
    new_place = 3 - 2 * side if second else 1

    def at(row):
        return pl.multiple_of(row * pairs, pairs)

    clear_edges(glob_taps, pairs)
    clear_edges(taps, pairs)
    for k, piece in enumerate(pieces):
        base = EDGE + at(place(away, k) * share)
        for m in range(pairs):
            value = piece[:, pl.ds(m * lanes, lanes)].astype(F32)
            glob_cells[pl.ds(base + m, share, stride=pairs), :] = value
    left, right = column_masks(CHUNK, lanes, pairs)
    lower = lax.broadcasted_iota(jnp.int32, (CHUNK, lanes), 1) < lanes // 2
    for start in range(0, half * pairs, CHUNK):
        here = glob_cells[pl.ds(EDGE + start, CHUNK), :]
        before = jnp.where(left, 0.0, glob_cells[pl.ds(EDGE - 1 + start, CHUNK), :])
        after = jnp.where(right, 0.0, glob_cells[pl.ds(EDGE + 1 + start, CHUNK), :])
        part = pl.ds(at(new_place + start // pairs), CHUNK)
        glob_taps[part, pl.ds(0, lanes)] = here.astype(BF16)
        glob_taps[part, pl.ds(lanes, lanes)] = jnp.where(lower, after, before).astype(BF16)
    if second:
        glob_taps[pl.ds(at(1 + half * side), 2 * pairs), :] = glob_edge[...]
        taps[pl.ds(at((half + 2) * side), 2 * pairs), :] = taps_edge[...]
    for low, count in row_parts(act_rows, pairs):
        size = count * pairs
        left, right = column_masks(size, out, pairs)
        value = acc_ref[pl.ds(at(act_first + low), size), :] + pair_taps(
            glob_taps, w_glob_ref, at(act_place + low - 1), size, pairs
        )
        value = silu(value)
        part = pl.ds(at(act_place + low), size)
        taps[part, pl.ds(out, 2 * out)] = value.astype(BF16)
        before = jnp.where(left, 0.0, pltpu.roll(value[:, out:], 1, 0))
        after = jnp.where(right, 0.0, pltpu.roll(value[:, :out], size - 1, 0))
        taps[part, pl.ds(0, out)] = before.astype(BF16)
        taps[part, pl.ds(3 * out, out)] = after.astype(BF16)
    if not second:
        glob_edge[...] = glob_taps[pl.ds(at(1 + (half - 2) * (1 - side)), 2 * pairs), :]
        taps_edge[...] = taps[pl.ds(at(2 + (half - 4) * (1 - side)), 2 * pairs), :]
    writes = []
    for low, count in row_parts(rows, pairs):
        size = count * pairs
        value = pair_taps(taps, w_second_ref, low * pairs, size, pairs)
        value = silu(value + lifted_ref[pl.ds(at(first + low), size), :])
        start = 2 * low * pairs
        cells[pl.ds(start, size, stride=2), :] = value[:, :out]
        cells[pl.ds(start + 1, size, stride=2), :] = value[:, out:]
        for here, count in ((low, count // 2), (low + count // 2, count - count // 2)):
            part = pl.ds(here, count)
            value = cells[pl.ds(here * width, count * width), :].reshape(count, width, channels)
            resident = x_ref[pl.ds(first + here, count), :, :].astype(F32)
            out_ref[part, :, :] = (resident + value).astype(BF16)
            writes += start_copies(
                [(out_ref.at[part, :, :], out_hbm.at[pl.ds(first + here, count), :, :])],
                sems.at[pl.ds(len(writes), 1)],
            )
    for write in writes:
        write.wait()


def rest_part(second, side_of, place, flags, acc, lifted, x, w_second, w_glob, pieces, carried):
    _, width, channels = x.shape
    pairs = width // 2
    lanes = pieces[0].shape[1] // pairs
    half = pieces[0].shape[0] * len(pieces)
    rows = half + 2 if second else half
    space = pltpu.with_memory_space_constraint
    results = (pltpu.HBM(x.shape, BF16),)
    if not second:
        results += (
            pltpu.VMEM((2 * pairs, 2 * lanes), BF16),
            pltpu.VMEM((2 * pairs, 4 * channels), BF16),
        )
    return pl.pallas_call(
        lambda *refs: rest_kernel(second, side_of, place, *refs),
        out_shape=results,
        in_specs=in_vmem(6 + len(pieces))
        + (in_vmem(2) + in_hbm(1) if second else []),
        out_specs=tuple(in_hbm(1) + in_vmem(len(results) - 1)),
        input_output_aliases={8 + len(pieces): 0} if second else {},
        scratch_shapes=[
            pltpu.VMEM((rows, width, channels), BF16),
            pltpu.VMEM(((half + 1) * pairs + 2 * EDGE, lanes), F32),
            pltpu.VMEM(((rows + 2) * pairs, 2 * lanes), BF16),
            pltpu.VMEM(((rows + 2) * pairs, 4 * channels), BF16),
            pltpu.VMEM((rows * width + EDGE, channels), F32),
            pltpu.SemaphoreType.DMA((2 * len(row_parts(rows, pairs)),)),
        ],
        compiler_params=pltpu.CompilerParams(vmem_limit_bytes=VMEM_BYTES),
        cost_estimate=pl.CostEstimate(
            flops=4 * rows * width * 12 * channels * channels,
            bytes_accessed=4 * 1024 * 1024,
            transcendentals=0,
        ),
        name="rest_second" if second else "rest_first",
    )(
        *(space(a, pltpu.VMEM) for a in (flags, acc, lifted, x, w_second, w_glob)),
        *pieces,
        *carried,
    )


def rotated(block, axis, distance):
    count = lax.axis_size(axis)
    return lax.ppermute(block, axis, [(i, (i + distance) % count) for i in range(count)])


def swapped(block, bit):
    count = lax.axis_size("patch")
    return lax.ppermute(block, "patch", [(i, i ^ bit) for i in range(count)])


def side_first(away):
    return (away ^ (away >> 1)) & 1


def place_first(away, k):
    return ((away >> 1) ^ k) & 1


def per_device(
    features, context, owner, hours, w_first, w_second, w_lead_in, w_lead_mix, w_lead_out
):
    resident, block = features[0, 0], context[0, 0]
    acc, proj, flags, kept, w_second, w_glob, resident = resident_part(
        owner, resident, w_first, w_second, w_lead_in, block
    )

    def lifted_with(proj):
        before, after = rotated(proj, "lead", 1), rotated(proj, "lead", -1)
        return mix_part(hours, before, proj, after, w_lead_mix, w_lead_out)

    def rest(second, side_of, place, lifted, pieces, carried):
        return rest_part(second, side_of, place, flags, acc, lifted, resident, w_second, w_glob, pieces, carried)

    if lax.axis_size("patch") != 4:
        mine = lax.axis_index("patch") == owner[lax.axis_index("lead")]
        whole = lax.psum(jnp.where(mine, block, jnp.zeros_like(block)), "patch")
        result, _, _ = rest(
            False, lambda away: 0, lambda away, k: k, lifted_with(proj), [whole], []
        )
        return result[None, None]

    near, beside = flags[0] == 0, flags[1] == 0
    half = block.shape[0] // 2
    share = half // 2
    passing = swapped(block[half + share :], 1)
    staying = swapped(block[half : half + share], 1)
    passing, proj = lax.optimization_barrier((passing, proj))
    passing = jnp.where(near, kept[share:], passing)
    staying = jnp.where(near, kept[:share], staying)
    own = jnp.where(beside, staying, swapped(passing, 3))
    across = swapped(own, 3)
    lifted = lifted_with(proj)
    upper = [own, across]
    lower = [swapped(own, 1), swapped(across, 1)]
    result, *edges = rest(False, side_first, place_first, lifted, upper, [])
    (result,) = rest(True, side_first, place_first, lifted, lower, [*edges, result])
    return result[None, None]


def solution(mesh):
    placed = (
        P(("grp", "lead"), "patch", None, None, None),
        P("patch", ("grp", "lead"), None, None),
        P("grp"),
        P("grp"),
        P(),
        P(),
        P(),
        P(),
        P(),
    )
    return jax.shard_map(
        per_device,
        mesh=mesh,
        in_specs=placed,
        out_specs=P(("grp", "lead"), "patch", None, None, None),
        check_vma=False,
    )
```
